32 devices in a mesh: ga: 2 (over y), aa: 4 (over x, core), ba: 4 (over z).
Axes of the slice: x: 2, y: 2, z: 4, core: 2. Of those that a mesh axis runs over, the one named last changes fastest.
Arguments:
- query: bfloat16 [2048, 5120], P(('ga', 'aa'), 'ba'), parts along dimension 0, may hold values from -64 to 64
- keys: bfloat16 [16384, 1024], P(('ga', 'aa'), 'ba'), parts along dimension 0, may hold values from -16 to 16
- values: bfloat16 [16384, 1024], P(('ga', 'aa'), 'ba'), parts along dimension 0, may hold values from -6 to 6
- cache_lengths: int32 [8], P(('ga', 'aa')), parts along dimension 0, may hold values from 256 to 2048, as said below
- residual: bfloat16 [2048, 5120], P(('ga', 'ba'), 'aa'), parts along dimension 0, may hold values from -16 to 16
- out_weight: bfloat16 [5120, 5120], P('ba', 'aa'), may hold values from -0.078125 to 0.078125
- norm_gain: float32 [5120], P('aa'), may hold values from 0.1 to 1.9
- router_weight: float32 [5120, 4], P('aa'), may hold values from -0.078125 to 0.078125
- expert_ids: int32 [2048], P(('ga', 'ba')), parts along dimension 0, may hold values from 0 to 3
- expert_slots: int32 [2048], P(('ga', 'ba')), parts along dimension 0, may hold values from -1 to 127, as said below
- expert_gate: bfloat16 [4, 5120, 4096], P('ba', None, 'aa'), may hold values from -0.078125 to 0.078125
- expert_up: bfloat16 [4, 5120, 4096], P('ba', None, 'aa'), may hold values from -0.078125 to 0.078125
- expert_down: bfloat16 [4, 4096, 5120], P('ba', 'aa'), may hold values from -0.25 to 0.25
Outputs:
- layer_out: bfloat16 [2048, 5120], P(('ga', 'ba'), 'aa'), parts along dimension 0
The draws below stay inside these ranges and needn't reach their ends.
There are 2 independent parts, one for each index of `ga`. The reference program is written for one: setup_inputs(seed, part) draws one part's arguments, and reference() takes and returns one part's arrays. A program takes and returns all parts, laid end to end along the dimension named above; an argument that names none is the same for every part. Nothing has to cross between parts.
Inputs may be any that keep to these rules, and one draw needn't show every extreme that they name: `cache_lengths`: some shard has 2048 valid positions in every draw. `expert_slots`: rows form aligned blocks of 256 rows (the rows of one index of ba). A row's slot is the number of earlier rows of its block with the same expert id, or -1 where that number is 128 or more. In every draw some expert has all 128 slots filled in every block.
All inputs are finite; a program needn't handle non-finite values.
Results may differ from the reference program's by a relative error of at most 0.019.
Values may be sent and summed in bfloat16 or wider, within the bound.
A program may use at most 128 MiB of HBM per device.

```python
import jax
import jax.numpy as jnp
from jax import lax

D = 5120
H = 40
KVH = 8
HD = 128
FF = 4096
EXP_DEV = 1
Q = 1024
CTX_DEV = 2048
CTX = 8192
EXPERTS = 4
CAPS = 128


def draw_keys(key, part):
    base = jax.random.normal(jax.random.fold_in(key, 3), (CTX, KVH * HD), jnp.float32)
    return jnp.clip(base, -16.0, 16.0).astype(jnp.bfloat16)


def draw_query(key, part):
    base = 3.0 * jax.random.normal(jax.random.fold_in(key, 7), (Q, H * HD), jnp.float32)
    return jnp.clip(base, -64.0, 64.0).astype(jnp.bfloat16)


def draw_residual(key, part):
    columns = jnp.arange(D, dtype=jnp.float32) / D
    base = jax.random.normal(jax.random.fold_in(key, 11), (Q, D), jnp.float32) * (0.4 * 4.0 ** columns)[None, :]
    return jnp.clip(base, -16.0, 16.0).astype(jnp.bfloat16)


def draw_cache_lengths(key, part):
    shards = CTX // CTX_DEV
    lengths = jax.random.randint(jax.random.fold_in(key, 41), (shards,), CTX_DEV // 8, CTX_DEV + 1)
    full = jax.random.randint(jax.random.fold_in(key, 42), (), 0, shards)
    return lengths.at[full].set(CTX_DEV).astype(jnp.int32)


def routing(key):
    base = jax.random.fold_in(key, 29)
    blocks = EXPERTS // EXP_DEV
    rows = Q // blocks
    first = jax.random.randint(jax.random.fold_in(base, 1), (blocks, rows), 0, EXPERTS)
    second = jax.random.randint(jax.random.fold_in(base, 2), (blocks, rows), 0, EXPERTS)
    order = jax.random.permutation(jax.random.fold_in(base, 3), EXPERTS)
    ids = order[jnp.minimum(first, second)]
    scores = jax.random.randint(jax.random.fold_in(base, 4), (blocks, rows), 0, 1 << 20) * rows + jnp.arange(rows, dtype=jnp.int32)[None, :]
    ranks = jnp.argsort(jnp.argsort(scores, axis=1), axis=1)
    ids = jnp.where(ranks < CAPS, order[0], ids)
    onehot = (ids[..., None] == jnp.arange(EXPERTS, dtype=jnp.int32)[None, None, :]).astype(jnp.int32)
    earlier = jnp.sum((jnp.cumsum(onehot, axis=1) - onehot) * onehot, axis=-1)
    slots = jnp.where(earlier < CAPS, earlier, -1)
    return (ids.reshape(Q).astype(jnp.int32), slots.reshape(Q).astype(jnp.int32))


def draw_expert_ids(key, part):
    return routing(key)[0]


def draw_expert_slots(key, part):
    return routing(key)[1]


def block_scale(own_key, shape, pieces, low, high):
    level, own = 1.0, jax.random.fold_in(own_key, 6)
    for axis_at, parts in pieces:
        steps = jnp.exp(jax.random.uniform(jax.random.fold_in(own, axis_at), (parts,), jnp.float32, low / len(pieces), high / len(pieces)))
        level = level * jnp.repeat(steps, shape[axis_at] // parts).reshape([-1 if axis == axis_at else 1 for axis in range(len(shape))])
    return level


def bell_draw(stream_key, extent, width, bound, cuts=(), held_as=jnp.bfloat16):
    entries = jax.random.normal(stream_key, extent, jnp.float32) * width
    if len(cuts) > 0:
        entries = block_scale(stream_key, extent, cuts, -0.22, 0.18) * entries
    return jnp.clip(entries, min=-bound, max=bound).astype(held_as)


def setup_inputs(seed: int = 0, part: int = 0) -> dict:
    splits = jax.random.split(jax.random.key(seed), 14)
    part_splits = jax.random.split(jax.random.fold_in(splits[13], part), 14)
    return {
        "query": draw_query(jax.random.fold_in(jax.random.fold_in(splits[13], part), 71), part),
        "keys": draw_keys(jax.random.fold_in(jax.random.fold_in(splits[13], part), 71), part),
        "values": bell_draw(part_splits[2], (CTX, KVH * HD), 1.0, 6.0, ((0, 4), (1, 4))),
        "cache_lengths": draw_cache_lengths(jax.random.fold_in(jax.random.fold_in(splits[13], part), 71), part),
        "residual": draw_residual(jax.random.fold_in(jax.random.fold_in(splits[13], part), 71), part),
        "out_weight": bell_draw(splits[5], (H * HD, D), (H * HD) ** -0.5, 0.078125, ((0, 4), (1, 4))),
        "norm_gain": jnp.clip(1.0 + 0.18 * jax.random.normal(splits[6], (D,), jnp.float32), 0.1, 1.9),
        "router_weight": bell_draw(splits[7], (D, EXPERTS), D ** -0.5, 0.078125, ((0, 4),), jnp.float32),
        "expert_ids": draw_expert_ids(jax.random.fold_in(jax.random.fold_in(splits[13], part), 71), part),
        "expert_slots": draw_expert_slots(jax.random.fold_in(jax.random.fold_in(splits[13], part), 71), part),
        "expert_gate": bell_draw(splits[10], (EXPERTS, D, FF), D ** -0.5, 0.078125, ((0, 4), (2, 4))),
        "expert_up": bell_draw(splits[11], (EXPERTS, D, FF), D ** -0.5, 0.078125, ((0, 4), (2, 4))),
        "expert_down": bell_draw(splits[12], (EXPERTS, FF, D), (FF // 8) ** -0.5, 0.25, ((0, 4), (1, 4))),
    }


NEGATIVE = -1e+30
EPSILON = 1e-05

def reference(query, keys, values, cache_lengths, residual, out_weight, norm_gain, router_weight, expert_ids, expert_slots, expert_gate, expert_up, expert_down):
    group = H // KVH
    shards = CTX // CTX_DEV
    queries = query.astype(jnp.float32).reshape(Q, KVH, group, HD)

    def one_shard(index):
        start = (index * CTX_DEV).astype(jnp.int32)
        key_block = lax.dynamic_slice_in_dim(keys, start, CTX_DEV, 0).astype(jnp.float32).reshape(CTX_DEV, KVH, HD)
        value_block = lax.dynamic_slice_in_dim(values, start, CTX_DEV, 0).astype(jnp.float32).reshape(CTX_DEV, KVH, HD)
        scores = jnp.einsum('qkgd,tkd->kgqt', queries, key_block) * HD ** (-0.5)
        valid = jnp.arange(CTX_DEV, dtype=jnp.int32) < cache_lengths[index]
        scores = jnp.where(valid, scores, NEGATIVE)
        peak = lax.optimization_barrier(jnp.max(scores, axis=-1))
        probs = jnp.exp(scores - peak[..., None])
        total = lax.optimization_barrier(jnp.sum(probs, axis=-1))
        rounded = lax.optimization_barrier(probs.astype(jnp.bfloat16)).astype(jnp.float32)
        weighted = jnp.einsum('kgqt,tkd->kgqd', rounded, value_block)
        return (peak, total, weighted)
    peaks, totals, outputs = lax.map(one_shard, jnp.arange(shards, dtype=jnp.int32))
    top = lax.optimization_barrier(jnp.max(peaks, axis=0))
    factor = jnp.exp(peaks - top)
    numer = lax.optimization_barrier(jnp.sum(factor[..., None] * outputs, axis=0))
    denom = lax.optimization_barrier(jnp.sum(factor * totals, axis=0))
    attended = (numer / denom[..., None]).transpose(2, 0, 1, 3).reshape(Q, H * HD).astype(jnp.bfloat16)
    hidden = residual.astype(jnp.float32) + jnp.dot(attended, out_weight, preferred_element_type=jnp.float32)
    inverse = 1.0 / jnp.sqrt(lax.optimization_barrier(jnp.mean(hidden * hidden, axis=1)) + EPSILON)
    normed = hidden * inverse[:, None] * norm_gain
    logits = jnp.dot(normed, router_weight, precision=lax.Precision.HIGHEST)
    chosen = expert_ids[:, None] == jnp.arange(EXPERTS, dtype=jnp.int32)[None, :]
    gate = lax.optimization_barrier(jnp.sum(jnp.where(chosen, jax.nn.sigmoid(logits), 0.0), axis=1))
    expert_in = normed.astype(jnp.bfloat16)
    blocks = EXPERTS // EXP_DEV
    rows = Q // blocks
    combined = expert_ids * CAPS + expert_slots
    select = (combined[:, None] == jnp.arange(EXPERTS * CAPS, dtype=jnp.int32)[None, :]) & (expert_slots[:, None] >= 0)
    select = select.astype(jnp.float32).reshape(blocks, rows, EXPERTS, CAPS)
    buffer = jnp.einsum('brec,brd->ebcd', select, expert_in.astype(jnp.float32).reshape(blocks, rows, D))
    buffer = buffer.reshape(EXPERTS, blocks * CAPS, D).astype(jnp.bfloat16)

    def one_expert(operands):
        slots_in, gate_w, up_w, down_w = operands
        gate_part = jnp.dot(slots_in, gate_w, preferred_element_type=jnp.float32)
        up_part = jnp.dot(slots_in, up_w, preferred_element_type=jnp.float32)
        act = (jax.nn.silu(gate_part) * up_part).astype(jnp.bfloat16)
        return jnp.dot(act, down_w, preferred_element_type=jnp.float32).astype(jnp.bfloat16)
    outbuf = lax.map(one_expert, (buffer, expert_gate, expert_up, expert_down))
    outbuf = outbuf.reshape(EXPERTS, blocks, CAPS, D).astype(jnp.float32)
    back = jnp.einsum('brec,ebcd->brd', select, outbuf).reshape(Q, D)
    return (hidden + gate[:, None] * back).astype(jnp.bfloat16)
```

```python
import functools

import jax
import jax.numpy as jnp
from jax import lax
from jax.experimental import pallas as pl
from jax.experimental.pallas import tpu as pltpu
from jax.sharding import PartitionSpec as P

D = 5120
HD = 128
Q = 1024
STEP = 1024
LOADS = 4
PARTS = 2
PROJECT_GRANT = 48 * 1024 * 1024
TILE = 256
EXPERTS_GRANT = 67043328
ATTEND_GRANT = 60 * 1024 * 1024
LANES = 128
LOG2E = 1.4426950408889634


NEGATIVE = -1e30
EPSILON = 1e-05


def attend_kernel(shards, group, lengths, q_ref, *refs):
    sources = refs[: 2 * shards]
    out_ref, stat_ref, kv_ref, stack_ref, peak_ref, acc_ref, sems = refs[2 * shards :]
    factor = HD ** (-0.5) * LOG2E
    rows = q_ref.shape[0]
    context = kv_ref.shape[2]
    step = min(STEP, context)
    tails = [size for size in (step // 2, step) if size % LANES == 0]
    g = pl.program_id(0)
    column = pl.ds(pl.multiple_of(g * HD, HD), HD)

    @pl.when(g == 0)
    def _():
        for at, source in enumerate(sources):
            pltpu.make_async_copy(source, kv_ref.at[at // 2, at % 2], sems.at[at // 2, at % 2]).start()

    for head in range(group):
        stack_ref[head * rows : (head + 1) * rows, :] = q_ref[:, head * HD : (head + 1) * HD]
    peak_ref[...] = jnp.full_like(peak_ref, NEGATIVE)
    acc_ref[...] = jnp.zeros_like(acc_ref)

    def chunk(shard, start, size, limit):
        k = kv_ref[shard, 0, pl.ds(start, size), column]
        v = kv_ref[shard, 1, pl.ds(start, size), column]
        v = jnp.concatenate([v, jnp.ones((size, HD), jnp.bfloat16)], axis=1)
        for head in range(group):
            span = slice(head * rows, (head + 1) * rows)
            scores = lax.dot_general(
                stack_ref[span, :], k, (((1,), (1,)), ((), ())), preferred_element_type=jnp.float32
            )
            if limit is not None:
                place = lax.broadcasted_iota(jnp.int32, scores.shape, 1)
                scores = jnp.where(place < limit, scores, NEGATIVE)
            old = peak_ref[span, :]
            new = jnp.maximum(old, jnp.max(scores, axis=1, keepdims=True))
            probs = jnp.exp2((scores - new[:, :1]) * factor).astype(jnp.bfloat16)
            scale = jnp.exp2((old - new) * factor)
            peak_ref[span, :] = new
            acc_ref[span, :] = acc_ref[span, :] * jnp.concatenate([scale, scale], axis=1) + jnp.dot(
                probs, v, preferred_element_type=jnp.float32
            )

    @pl.loop(0, shards)
    def _(shard):
        @pl.when(g == 0)
        def _():
            for part in range(2):
                pltpu.make_async_copy(
                    sources[part], kv_ref.at[shard, part], sems.at[shard, part]
                ).wait()

        length = lengths[shard]
        full = length // step
        left = length - full * step
        start = pl.multiple_of(full * step, step)

        @pl.loop(0, full)
        def _(i):
            chunk(shard, pl.multiple_of(i * step, step), step, None)

        low = 0
        for size in tails:

            @pl.when((left > low) & (left <= size))
            def _(size=size):
                chunk(shard, start, size, left)

            low = size

    for head in range(group):
        span = slice(head * rows, (head + 1) * rows)
        out_ref[:, head * HD : (head + 1) * HD] = (acc_ref[span, :HD] / acc_ref[span, HD:]).astype(
            out_ref.dtype
        )
        stat_ref[0, 0, head : head + 1, :] = jnp.transpose(peak_ref[span, :])[0:1, :]
        stat_ref[0, 1, head : head + 1, :] = jnp.transpose(acc_ref[span, HD:])[0:1, :]


def attend(query, key_blocks, value_blocks, lengths, out_type):
    shards = len(key_blocks)
    rows, width = query.shape
    context, kv_width = key_blocks[0].shape
    kv_heads = kv_width // HD
    group = width // HD // kv_heads
    work = shards * rows * width * context
    sources = [array for pair in zip(key_blocks, value_blocks) for array in pair]
    return pl.pallas_call(
        functools.partial(attend_kernel, shards, group),
        grid_spec=pltpu.PrefetchScalarGridSpec(
            num_scalar_prefetch=1,
            grid=(kv_heads,),
            in_specs=[pl.BlockSpec((rows, group * HD), lambda g, n: (0, g))]
            + [pl.BlockSpec(memory_space=pl.ANY)] * (2 * shards),
            out_specs=[
                pl.BlockSpec((rows, group * HD), lambda g, n: (0, g)),
                pl.BlockSpec((1, 2, group, rows), lambda g, n: (g, 0, 0, 0)),
            ],
            scratch_shapes=[
                pltpu.VMEM((shards, 2, context, kv_width), jnp.bfloat16),
                pltpu.VMEM((group * rows, HD), jnp.bfloat16),
                pltpu.VMEM((group * rows, HD), jnp.float32),
                pltpu.VMEM((group * rows, 2 * HD), jnp.float32),
                pltpu.SemaphoreType.DMA((shards, 2)),
            ],
        ),
        out_shape=[
            jax.ShapeDtypeStruct((rows, width), out_type),
            jax.ShapeDtypeStruct((kv_heads, 2, group, rows), jnp.float32),
        ],
        cost_estimate=pl.CostEstimate(
            flops=4 * work, bytes_accessed=4 * shards * context * kv_heads * HD + 6 * rows * width,
            transcendentals=work // HD,
        ),
        compiler_params=pltpu.CompilerParams(vmem_limit_bytes=ATTEND_GRANT),
        name="attend",
    )(lengths, query, *sources)


def span_attention(query, keys, values, cache_lengths):
    size = lax.axis_size("aa")
    swap = [(i, i ^ 1) for i in range(size)]
    far = []
    for hop in range(2, size, 2):
        ahead = [(i, (i + hop) % size) for i in range(size)]
        far.append((lax.ppermute(query, "aa", ahead), [(j, i) for i, j in ahead]))
    near_keys = lax.ppermute(keys, "aa", swap)
    near_values = lax.ppermute(values, "aa", swap)
    near_length = lax.ppermute(cache_lengths, "aa", swap)
    both = jnp.concatenate([cache_lengths, near_length])
    parts = [attend(query, [keys], [values], cache_lengths, jnp.float32)]
    for rows, back in far:
        rows, parts[0] = lax.optimization_barrier((rows, parts[0]))
        out, stat = attend(rows, [keys, near_keys], [values, near_values], both, jnp.bfloat16)
        parts.append((lax.ppermute(out, "aa", back), lax.ppermute(stat, "aa", back)))
    parts.append(attend(query, [near_keys], [near_values], near_length, jnp.float32))
    return merge(parts, keys.shape[1] // HD)


def merge_kernel(count, group, *refs):
    stats, outs, out_ref = refs[:count], refs[count : 2 * count], refs[-1]
    factor = HD ** (-0.5) * LOG2E
    rows = out_ref.shape[0]
    top = functools.reduce(jnp.maximum, [stat[0, 0] for stat in stats])
    weights = [stat[0, 1] * jnp.exp2((stat[0, 0] - top) * factor) for stat in stats]
    whole = functools.reduce(jnp.add, weights)
    shares = [weight / whole for weight in weights]
    for head in range(group):
        span = slice(head * HD, (head + 1) * HD)
        terms = [
            out[:, span].astype(jnp.float32)
            * jnp.transpose(jnp.broadcast_to(share[head : head + 1, :], (HD, rows)))
            for out, share in zip(outs, shares)
        ]
        out_ref[:, span] = functools.reduce(jnp.add, terms).astype(out_ref.dtype)


def merge(parts, kv_heads):
    count = len(parts)
    rows, width = parts[0][0].shape
    group = width // HD // kv_heads
    wide = pl.BlockSpec((rows, group * HD), lambda g: (0, g))
    return pl.pallas_call(
        functools.partial(merge_kernel, count, group),
        grid=(kv_heads,),
        in_specs=[pl.BlockSpec((1, 2, group, rows), lambda g: (g, 0, 0, 0))] * count + [wide] * count,
        out_specs=wide,
        out_shape=jax.ShapeDtypeStruct((rows, width), jnp.bfloat16),
        name="merge",
    )(*[stat for _, stat in parts], *[out for out, _ in parts])


def peers_of(me_a, me_b, n, m):
    peers = [{"ba": lax.rem(me_b + k, m)} for k in range(1, m)]
    peers += [{"aa": lax.rem(me_a + hop, n)} for hop in range(2, n, 2)]
    return peers + [{"aa": partner_of(me_a)}]


def partner_of(me_a):
    return me_a + 1 - 2 * lax.rem(me_a, 2)


def meet(peers):
    barrier = pltpu.get_barrier_semaphore()
    for peer in peers:
        pl.semaphore_signal(barrier, inc=1, device_id=peer, device_id_type=pl.DeviceIdType.MESH)
    pl.semaphore_wait(barrier, len(peers))


def remote(source, target, send, receive, peer):
    copy = pltpu.make_async_remote_copy(
        src_ref=source,
        dst_ref=target,
        send_sem=send,
        recv_sem=receive,
        device_id=peer,
        device_id_type=pl.DeviceIdType.MESH,
    )
    copy.start()
    return copy


def dispatch_kernel(local, n, m, packed, out, own_sem, z_send, z_recv, x_send, x_recv, c_send, c_recv):
    me_a, me_b = lax.axis_index("aa"), lax.axis_index("ba")
    slots, columns = packed.shape[1], packed.shape[2]
    meet(peers_of(me_a, me_b, n, 1 if local else m))

    def index(k):
        return k if local else lax.rem(me_b - k + m, m)

    def place(b, a):
        if len(out.shape) == 3:
            return out.at[a, pl.ds(pl.multiple_of(b * slots, slots), slots)]
        return out.at[
            pl.ds(pl.multiple_of(b * slots, slots), slots),
            pl.ds(pl.multiple_of(a * columns, columns), columns),
        ]

    own = []
    for k in range(m if local else 1):
        own.append(pltpu.make_async_copy(packed.at[index(k)], place(index(k), me_a), own_sem.at[k]))
        own[k].start()
    over_z = [None]
    for k in range(1, 1 if local else m):
        to = lax.rem(me_b + k, m)
        over_z.append(
            remote(packed.at[to], place(me_b, me_a), z_send.at[k], z_recv.at[k], {"ba": to})
        )
    partner = partner_of(me_a)
    over_x, over_c = {}, {}

    def forward(k):
        b = index(k)
        for j, hop in enumerate(range(2, n, 2), 1):
            over_x[k, j].wait_recv()
            block = place(b, lax.rem(me_a - hop + n, n))
            over_c[k, j] = remote(
                block, block, c_send.at[k, j], c_recv.at[k, j], {"aa": partner}
            )

    for k in range(m):
        if k < len(own):
            own[k].wait()
        else:
            over_z[k].wait_recv()
        block = place(index(k), me_a)
        for j, hop in enumerate(range(2, n, 2), 1):
            over_x[k, j] = remote(
                block,
                block,
                x_send.at[k, j],
                x_recv.at[k, j],
                {"aa": lax.rem(me_a + hop, n)},
            )
        over_c[k, 0] = remote(block, block, c_send.at[k, 0], c_recv.at[k, 0], {"aa": partner})
        if k > 0:
            forward(k - 1)
    forward(m - 1)
    for copy in over_c.values():
        copy.wait_recv()
    for copy in over_z[1:] + list(over_x.values()) + list(over_c.values()):
        copy.wait_send()


def dispatch(packed, local, m, name, number):
    n = lax.axis_size("aa")
    columns = packed.shape[1]
    rows = packed.shape[0] // m
    half = n // 2
    sems = [pltpu.SemaphoreType.DMA((m,))] * 2 + [pltpu.SemaphoreType.DMA((m, half))] * 4
    flat = columns % LANES == 0 and not local
    shape = (m * rows, n * columns) if flat else (n, m * rows, columns)
    out = pl.pallas_call(
        functools.partial(dispatch_kernel, local, n, m),
        out_shape=jax.ShapeDtypeStruct(shape, packed.dtype),
        in_specs=[pl.BlockSpec(memory_space=pltpu.VMEM)],
        out_specs=pl.BlockSpec(memory_space=pltpu.VMEM),
        scratch_shapes=[pltpu.SemaphoreType.DMA((m,))] + sems,
        compiler_params=pltpu.CompilerParams(
            collective_id=number, has_side_effects=True, vmem_limit_bytes=24 * 1024 * 1024
        ),
        name=name,
    )(packed.reshape(m, rows, columns))
    if local:
        return out.reshape(n * m * rows, columns)
    return out if flat else out.transpose(1, 0, 2).reshape(m * rows, n * columns)


def combine_kernel(
    n, m, part, out, near, summed, far, total, own_sem, z_send, z_recv, x_send, x_recv, c_send, c_recv
):
    me_a, me_b = lax.axis_index("aa"), lax.axis_index("ba")
    slots, columns = out.shape[1], out.shape[2]
    meet(peers_of(me_a, me_b, n, m))
    partner = partner_of(me_a)

    def piece(k, a):
        b = lax.rem(me_b + k, m)
        if len(part.shape) == 3:
            return part.at[a, pl.ds(pl.multiple_of(b * slots, slots), slots)]
        return part.at[
            pl.ds(pl.multiple_of(b * slots, slots), slots),
            pl.ds(pl.multiple_of(a * columns, columns), columns),
        ]

    order = list(range(1, m)) + [0]
    over_c, over_x = {}, {}
    over_z = [None] * m
    for k in order:
        for j in range(n // 2):
            over_c[k, j] = remote(
                piece(k, lax.rem(partner + 2 * j, n)),
                near.at[k, j],
                c_send.at[k, j],
                c_recv.at[k, j],
                {"aa": partner},
            )

    def join(k, j):
        over_c[k, j].wait_recv()
        mine = piece(k, lax.rem(me_a + 2 * j, n))
        return mine[...].astype(jnp.float32) + near[k, j].astype(jnp.float32)

    def finish(k):
        value = join(k, 0)
        for j in range(1, n // 2):
            over_x[k, j].wait_recv()
            value = value + far[k, j].astype(jnp.float32)
        total[k] = value.astype(total.dtype)
        if k == 0:
            copy = pltpu.make_async_copy(total.at[0], out.at[me_b], own_sem)
            copy.start()
            copy.wait()
        else:
            over_z[k] = remote(
                total.at[k],
                out.at[me_b],
                z_send.at[k],
                z_recv.at[k],
                {"ba": lax.rem(me_b + k, m)},
            )

    for k in order:
        for j in range(1, n // 2):
            summed[k, j] = join(k, j).astype(summed.dtype)
            over_x[k, j] = remote(
                summed.at[k, j],
                far.at[k, j],
                x_send.at[k, j],
                x_recv.at[k, j],
                {"aa": lax.rem(me_a + 2 * j, n)},
            )
    for k in order:
        finish(k)
    for copy in over_z[1:]:
        copy.wait_recv()
    for copy in over_z[1:] + list(over_x.values()) + list(over_c.values()):
        copy.wait_send()


def combine(part):
    n, m = lax.axis_size("aa"), lax.axis_size("ba")
    rows, columns = part.shape[0] // m, part.shape[1] // n
    if columns % LANES:
        part = part.reshape(m * rows, n, columns).transpose(1, 0, 2)
    half = n // 2
    sems = [pltpu.SemaphoreType.DMA((m,))] * 2 + [pltpu.SemaphoreType.DMA((m, half))] * 4
    block = pltpu.VMEM((m, half, rows, columns), part.dtype)
    out = pl.pallas_call(
        functools.partial(combine_kernel, n, m),
        out_shape=jax.ShapeDtypeStruct((m, rows, columns), part.dtype),
        in_specs=[pl.BlockSpec(memory_space=pltpu.VMEM)],
        out_specs=pl.BlockSpec(memory_space=pltpu.VMEM),
        scratch_shapes=[block, block, block, pltpu.VMEM((m, rows, columns), part.dtype)]
        + [pltpu.SemaphoreType.DMA]
        + sems,
        compiler_params=pltpu.CompilerParams(
            collective_id=2, has_side_effects=True, vmem_limit_bytes=40 * 1024 * 1024
        ),
        name="combine",
    )(part)
    return out.reshape(m * rows, columns)


def experts_kernel(
    n,
    m,
    packed,
    gate_hbm,
    up_hbm,
    down_hbm,
    out,
    inputs,
    gate_w,
    up_w,
    down_w,
    act,
    part,
    near,
    summed,
    far,
    total,
    load_sem,
    own_sem,
    z_send,
    z_recv,
    x_send,
    x_recv,
    c_send,
    c_recv,
    f_send,
    f_recv,
    bz_send,
    bz_recv,
    bx_send,
    bx_recv,
    bc_send,
    bc_recv,
):
    me_a, me_b = lax.axis_index("aa"), lax.axis_index("ba")
    slots, columns = packed.shape[1], packed.shape[2]
    width = n * columns
    hidden = gate_w.shape[1]
    across, partner = flip(me_a, 2), flip(me_a, 1)
    order = [0, 2, 1, 3]
    block_of = [flip(me_b, way) for way in order]

    loads = []
    for at, (source, target) in enumerate(
        ((gate_hbm, gate_w), (up_hbm, up_w), (down_hbm, down_w))
    ):
        piece = target.shape[0] // LOADS
        for i in range(LOADS):
            rows = pl.ds(i * piece, piece)
            loads.append(
                pltpu.make_async_copy(source.at[0, rows], target.at[rows], load_sem.at[at, i])
            )
            loads[-1].start()
    meet([{"ba": block_of[k]} for k in range(1, m)] + [{"aa": across}, {"aa": partner}])

    def place(k, a):
        return inputs.at[
            k * slots : (k + 1) * slots, pl.ds(pl.multiple_of(a * columns, columns), columns)
        ]

    over_z, over_x, over_c, over_f = {}, {}, {}, {}
    own = pltpu.make_async_copy(packed.at[me_b], place(0, me_a), own_sem)
    for k in range(1, m):
        over_z[k] = remote(
            packed.at[block_of[k]], place(k, me_a), z_send.at[k], z_recv.at[k], {"ba": block_of[k]}
        )

    def spread(k):
        if k:
            over_z[k].wait_recv()
        block = place(k, me_a)
        source = block if k else packed.at[me_b]
        over_x[k] = remote(source, block, x_send.at[k], x_recv.at[k], {"aa": across})
        over_c[k] = remote(source, block, c_send.at[k], c_recv.at[k], {"aa": partner})

    def forward(k):
        over_x[k].wait_recv()
        block = place(k, across)
        over_f[k] = remote(block, block, f_send.at[k], f_recv.at[k], {"aa": partner})

    def arrive(k):
        if k == 0:
            own.wait()
        over_c[k].wait_recv()
        over_f[k].wait_recv()

    def activate(pair, half):
        rows = slice(2 * pair * slots, 2 * (pair + 1) * slots)

        @pl.loop(0, hidden // 2 // TILE)
        def _(i):
            span = pl.ds(pl.multiple_of(half * (hidden // 2) + i * TILE, TILE), TILE)
            x = inputs[rows, :]
            gate = jnp.dot(x, gate_w[:, span], preferred_element_type=jnp.float32)
            up = jnp.dot(x, up_w[:, span], preferred_element_type=jnp.float32)
            act[rows, span] = (jax.nn.silu(gate) * up).astype(jnp.bfloat16)

    back_c, back_x, back_z = {}, {}, {}

    def lower(pair, a):
        rows = slice(2 * pair * slots, 2 * (pair + 1) * slots)
        span = pl.ds(pl.multiple_of(a * columns, columns), columns)
        part[rows, span] = jnp.dot(
            act[rows, :], down_w[:, span], preferred_element_type=jnp.float32
        ).astype(jnp.bfloat16)

    def piece(k, a):
        return part.at[
            k * slots : (k + 1) * slots, pl.ds(pl.multiple_of(a * columns, columns), columns)
        ]

    def hand(k, j, a):
        back_c[k, j] = remote(
            piece(k, a), near.at[k, j], bc_send.at[k, j], bc_recv.at[k, j], {"aa": partner}
        )

    def join(k, j, a):
        back_c[k, j].wait_recv()
        return piece(k, a)[...].astype(jnp.float32) + near[k, j].astype(jnp.float32)

    def cross(k):
        summed[k] = join(k, 1, across).astype(summed.dtype)
        back_x[k] = remote(
            summed.at[k], far.at[k], bx_send.at[k], bx_recv.at[k], {"aa": across}
        )

    def finish(k):
        value = join(k, 0, me_a)
        back_x[k].wait_recv()
        value = value + far[k].astype(jnp.float32)
        if k == 0:
            out[me_b] = value.astype(out.dtype)
        else:
            total[k] = value.astype(total.dtype)
            back_z[k] = remote(
                total.at[k], out.at[me_b], bz_send.at[k], bz_recv.at[k], {"ba": block_of[k]}
            )

    def descend(pair):
        first, second = 2 * pair + 1, 2 * pair
        lower(pair, flip(partner, 2))
        hand(first, 1, flip(partner, 2))
        hand(second, 1, flip(partner, 2))
        lower(pair, across)
        cross(first)
        cross(second)
        lower(pair, partner)
        hand(first, 0, partner)
        hand(second, 0, partner)
        lower(pair, me_a)

    spread(0)
    own.start()
    forward(0)
    spread(1)
    spread(2)
    forward(1)
    for copy in loads[: 2 * LOADS]:
        copy.wait()
    arrive(0)
    arrive(1)
    activate(0, 0)
    spread(3)
    forward(2)
    activate(0, 1)
    for copy in loads[2 * LOADS :]:
        copy.wait()
    descend(0)
    forward(3)
    arrive(2)
    arrive(3)
    activate(1, 0)
    finish(1)
    finish(0)
    activate(1, 1)
    descend(1)
    finish(3)
    finish(2)
    for copy in back_z.values():
        copy.wait_recv()
    for group in (over_z, over_x, over_c, over_f, back_c, back_x, back_z):
        for copy in group.values():
            copy.wait_send()


def flip(index, way):
    for bit in (1, 2):
        if way & bit:
            index = index + bit - 2 * bit * lax.rem(index // bit, 2)
    return index


def run_experts(packed, gate_w, up_w, down_w):
    n, m = lax.axis_size("aa"), lax.axis_size("ba")
    rows, columns = packed.shape[1:]
    depth, hidden = gate_w.shape[1:]
    block = pltpu.VMEM((m, rows, columns), jnp.bfloat16)
    one, two = pltpu.SemaphoreType.DMA((m,)), pltpu.SemaphoreType.DMA((m, 2))
    out = pl.pallas_call(
        functools.partial(experts_kernel, n, m),
        out_shape=jax.ShapeDtypeStruct((m, rows, columns), jnp.bfloat16),
        in_specs=[pl.BlockSpec(memory_space=pltpu.VMEM)]
        + [pl.BlockSpec(memory_space=pl.ANY)] * 3,
        out_specs=pl.BlockSpec(memory_space=pltpu.VMEM),
        scratch_shapes=[
            pltpu.VMEM((m * rows, n * columns), jnp.bfloat16),
            pltpu.VMEM((depth, hidden), jnp.bfloat16),
            pltpu.VMEM((depth, hidden), jnp.bfloat16),
            pltpu.VMEM((hidden, n * columns), jnp.bfloat16),
            pltpu.VMEM((m * rows, hidden), jnp.bfloat16),
            pltpu.VMEM((m * rows, n * columns), jnp.bfloat16),
            pltpu.VMEM((m, 2, rows, columns), jnp.bfloat16),
            block,
            block,
            block,
            pltpu.SemaphoreType.DMA((3, LOADS)),
            pltpu.SemaphoreType.DMA,
        ]
        + [one] * 12
        + [two] * 2,
        compiler_params=pltpu.CompilerParams(
            collective_id=1, has_side_effects=True, vmem_limit_bytes=EXPERTS_GRANT
        ),
        name="experts",
    )(packed, gate_w, up_w, down_w)
    return out.reshape(m * rows, columns)


def plain_experts(packed, gate_w, up_w, down_w):
    piece = dispatch(packed, False, lax.axis_size("ba"), "dispatch", 1)
    gate_part = jnp.dot(piece, gate_w, preferred_element_type=jnp.float32)
    up_part = jnp.dot(piece, up_w, preferred_element_type=jnp.float32)
    act = (jax.nn.silu(gate_part) * up_part).astype(jnp.bfloat16)
    return combine(jnp.dot(act, down_w, preferred_element_type=jnp.float32).astype(jnp.bfloat16))


def project_kernel(
    n,
    m,
    own,
    weight_hbm,
    residual_hbm,
    gain,
    router,
    ids,
    places,
    hidden,
    packed,
    gate,
    rows_in,
    weight,
    residual,
    up,
    down,
    leaving,
    value,
    stats,
    normed,
    load_sem,
    x_send,
    x_recv,
    c_send,
    c_recv,
    f_send,
    f_recv,
    u_send,
    u_recv,
    d_send,
    d_recv,
    s_send,
    s_recv,
):
    me_a, me_b = lax.axis_index("aa"), lax.axis_index("ba")
    rows, columns = hidden.shape
    experts = router.shape[0]
    slots = packed.shape[1]
    part = rows // PARTS
    across, partner = flip(me_a, 2), flip(me_a, 1)
    loads = [
        pltpu.make_async_copy(weight_hbm, weight, load_sem.at[0]),
        pltpu.make_async_copy(residual_hbm, residual, load_sem.at[1]),
        pltpu.make_async_copy(own, rows_in.at[0], load_sem.at[2]),
    ]
    for copy in loads:
        copy.start()
    meet(
        [{"ba": lax.rem(me_b + k, m)} for k in range(1, m)]
        + [{"aa": flip(me_a, way)} for way in range(1, n)]
    )

    def cut(c):
        return pl.ds(c * part, part)

    over_x, over_c, over_f = [], [], []
    for c in range(PARTS):
        block = own.at[cut(c)]
        over_x.append(
            remote(block, rows_in.at[2, cut(c)], x_send.at[c], x_recv.at[c], {"aa": across})
        )
    for c in range(PARTS):
        block = own.at[cut(c)]
        over_c.append(
            remote(block, rows_in.at[1, cut(c)], c_send.at[c], c_recv.at[c], {"aa": partner})
        )
    half, low = me_b // 2, lax.rem(me_b, 2)
    order = [3 - 3 * half, 2 - half, 2 * half + 1 - low, me_b]

    def climb(b, c, target):
        return pltpu.make_async_remote_copy(
            src_ref=leaving.at[b, cut(c)],
            dst_ref=up.at[b, cut(c)],
            send_sem=u_send.at[b, c],
            recv_sem=u_recv.at[b, c],
            device_id={"ba": target},
            device_id_type=pl.DeviceIdType.MESH,
        )

    def sink(b, c, target):
        return pltpu.make_async_remote_copy(
            src_ref=leaving.at[b, cut(c)],
            dst_ref=down.at[b, cut(c)],
            send_sem=d_send.at[b, c],
            recv_sem=d_recv.at[b, c],
            device_id={"ba": target},
            device_id_type=pl.DeviceIdType.MESH,
        )

    above, below = lax.rem(me_b + 1, m), lax.rem(me_b + m - 1, m)
    for copy in (loads[2], loads[0]):
        copy.wait()

    def step(at, c):
        b = order[at]
        slot = lax.rem(b // 2 + me_a // 2, 2) * 2 + lax.rem(b + me_a, 2)
        value[...] = jnp.dot(
            rows_in[slot, cut(c), :], weight[...], preferred_element_type=jnp.float32
        )

        @pl.when((b >= me_b) & (me_b > 0))
        def _():
            climb(b, c, above).wait_recv()
            value[...] += up[b, cut(c), :].astype(jnp.float32)

        @pl.when((b <= me_b) & (me_b < m - 1))
        def _():
            sink(b, c, below).wait_recv()
            value[...] += down[b, cut(c), :].astype(jnp.float32)

        if at == m - 1:
            hidden[cut(c), :] = residual[cut(c), :].astype(jnp.float32) + value[...]
            return
        leaving[b, cut(c), :] = value[...].astype(leaving.dtype)

        @pl.when(b > me_b)
        def _():
            climb(b, c, above).start()

        @pl.when(b < me_b)
        def _():
            sink(b, c, below).start()

    for c in range(PARTS):
        over_x[c].wait_recv()
        block = rows_in.at[2, cut(c)]
        over_f.append(
            remote(block, rows_in.at[3, cut(c)], f_send.at[c], f_recv.at[c], {"aa": partner})
        )
        over_c[c].wait_recv()
        over_f[c].wait_recv()
        step(0, c)
    for c in range(PARTS):
        step(1, c)
        step(2, c)
    loads[1].wait()
    for c in range(PARTS):
        step(3, c)

    lane = lax.broadcasted_iota(jnp.int32, (rows, LANES), 1)
    own_sum = jnp.sum(hidden[...] * hidden[...], axis=1, keepdims=True)
    mix = jnp.where(lane == experts, own_sum, 0.0)
    for e in range(experts):
        logit = jnp.sum(
            hidden[...] * gain[...] * router[e : e + 1, :], axis=1, keepdims=True
        )
        mix = jnp.where(lane == e, logit, mix)
    stats[0] = jnp.transpose(mix)[: stats.shape[1], :]
    over_s = [
        remote(
            stats.at[0],
            stats.at[way],
            s_send.at[way],
            s_recv.at[way],
            {"aa": flip(me_a, way)},
        )
        for way in range(1, n)
    ]
    place = jnp.where(places[...] >= 0, ids[...] * slots + places[...], -1)
    count = m * slots
    placing = (lax.broadcasted_iota(jnp.int32, (count, rows), 0) == place).astype(jnp.bfloat16)
    for copy in over_s:
        copy.wait_recv()
    sums = functools.reduce(jnp.add, [stats[way] for way in range(n)])
    inverse = 1.0 / jnp.sqrt(sums[experts : experts + 1, :] / (n * columns) + EPSILON)
    chosen = ids[...] == lax.broadcasted_iota(jnp.int32, (experts, rows), 0)
    gate[...] = jnp.sum(
        jnp.where(chosen, jax.nn.sigmoid(sums[:experts, :] * inverse), 0.0), axis=0, keepdims=True
    )
    spread = jnp.transpose(jnp.broadcast_to(inverse, (LANES, rows)))
    for at in range(0, columns, LANES):
        span = slice(at, at + LANES)
        normed[:, span] = (hidden[:, span] * spread * gain[:, span]).astype(jnp.bfloat16)
    for b in range(m):
        packed[b] = jnp.dot(
            placing[b * slots : (b + 1) * slots, :],
            normed[...],
            preferred_element_type=jnp.float32,
        ).astype(packed.dtype)
    for group in (over_x, over_c, over_f, over_s):
        for copy in group:
            copy.wait_send()
    for at in range(m - 1):
        for c in range(PARTS):

            @pl.when(order[at] > me_b)
            def _(b=order[at], c=c):
                climb(b, c, above).wait_send()

            @pl.when(order[at] < me_b)
            def _(b=order[at], c=c):
                sink(b, c, below).wait_send()


def project(own, weight, residual, gain, router, ids, places):
    n, m = lax.axis_size("aa"), lax.axis_size("ba")
    rows, columns = residual.shape
    experts = router.shape[1]
    slots = 2 * rows // experts
    block = pltpu.VMEM((m, rows, columns), jnp.bfloat16)
    one, two = pltpu.SemaphoreType.DMA((PARTS,)), pltpu.SemaphoreType.DMA((m, PARTS))
    vmem, anywhere = pl.BlockSpec(memory_space=pltpu.VMEM), pl.BlockSpec(memory_space=pl.ANY)
    return pl.pallas_call(
        functools.partial(project_kernel, n, m),
        out_shape=[
            jax.ShapeDtypeStruct((rows, columns), jnp.float32),
            jax.ShapeDtypeStruct((m, slots, columns), jnp.bfloat16),
            jax.ShapeDtypeStruct((1, rows), jnp.float32),
        ],
        in_specs=[vmem, anywhere, anywhere, vmem, vmem, vmem, vmem],
        out_specs=[vmem] * 3,
        scratch_shapes=[
            pltpu.VMEM((n, rows, own.shape[1]), jnp.bfloat16),
            pltpu.VMEM(weight.shape, jnp.bfloat16),
            pltpu.VMEM((rows, columns), jnp.bfloat16),
            block,
            block,
            block,
            pltpu.VMEM((rows // PARTS, columns), jnp.float32),
            pltpu.VMEM((n, 8, rows), jnp.float32),
            pltpu.VMEM((rows, columns), jnp.bfloat16),
            pltpu.SemaphoreType.DMA((3,)),
        ]
        + [one] * 6
        + [two] * 4
        + [pltpu.SemaphoreType.DMA((n,))] * 2,
        compiler_params=pltpu.CompilerParams(
            collective_id=4, has_side_effects=True, vmem_limit_bytes=PROJECT_GRANT
        ),
        name="project",
    )(
        own,
        weight,
        residual,
        gain.reshape(1, columns),
        router.T,
        ids.reshape(1, rows),
        places.reshape(1, rows),
    )


def placing_of(expert_ids, expert_slots, experts):
    slot_count = 2 * expert_ids.shape[0] // experts
    combined = expert_ids * slot_count + expert_slots
    placing = (
        combined[:, None] == lax.broadcasted_iota(jnp.int32, (1, experts * slot_count), 1)
    ) & (expert_slots[:, None] >= 0)
    return placing.astype(jnp.bfloat16)


def plain_project(
    own, out_weight, residual, norm_gain, router_weight, expert_ids, expert_slots
):
    attended = dispatch(own, True, 4 if own.shape[0] % 64 == 0 else 1, "gather", 3)
    hidden = residual.astype(jnp.float32) + lax.psum_scatter(
        jnp.dot(attended, out_weight, preferred_element_type=jnp.float32).astype(jnp.bfloat16),
        "ba",
        scatter_dimension=0,
        tiled=True,
    ).astype(jnp.float32)
    scaled = hidden * norm_gain
    sums = lax.psum(
        jnp.concatenate(
            [
                jnp.dot(scaled, router_weight, precision=lax.Precision.HIGHEST),
                jnp.sum(hidden * hidden, axis=1, keepdims=True),
            ],
            axis=1,
        ),
        "aa",
    )
    inverse = 1.0 / jnp.sqrt(sums[:, -1] / D + EPSILON)
    normed = scaled * inverse[:, None]
    logits = sums[:, :-1] * inverse[:, None]
    experts = router_weight.shape[1]
    chosen = expert_ids[:, None] == lax.broadcasted_iota(jnp.int32, (1, experts), 1)
    gate = jnp.sum(jnp.where(chosen, jax.nn.sigmoid(logits), 0.0), axis=1)
    expert_in = normed.astype(jnp.bfloat16)
    placing = placing_of(expert_ids, expert_slots, experts)
    packed = lax.dot_general(
        placing, expert_in, (((0,), (0,)), ((), ())), preferred_element_type=jnp.float32
    ).astype(jnp.bfloat16)
    return hidden, packed, gate


def on_device(
    query,
    keys,
    values,
    cache_lengths,
    residual,
    out_weight,
    norm_gain,
    router_weight,
    expert_ids,
    expert_slots,
    expert_gate,
    expert_up,
    expert_down,
):
    own = span_attention(query, keys, values, cache_lengths)
    n, m = lax.axis_size("aa"), lax.axis_size("ba")
    experts = router_weight.shape[1]
    rows, columns = residual.shape
    if n == 4 and m == 4 and experts == m and own.shape[0] == rows and columns % LANES == 0:
        hidden, packed, gate = project(
            own, out_weight, residual, norm_gain, router_weight, expert_ids, expert_slots
        )
        returned = run_experts(packed, expert_gate, expert_up, expert_down)
        gate = gate[0]
    else:
        hidden, packed, gate = plain_project(
            own, out_weight, residual, norm_gain, router_weight, expert_ids, expert_slots
        )
        returned = plain_experts(packed, expert_gate[0], expert_up[0], expert_down[0])
    placing = placing_of(expert_ids, expert_slots, experts)
    from_experts = jnp.dot(placing, returned, preferred_element_type=jnp.float32)
    return (hidden + gate[:, None] * from_experts).astype(jnp.bfloat16)


def solution(mesh):
    return jax.shard_map(
        on_device,
        mesh=mesh,
        in_specs=(
            P(("ga", "aa"), "ba"),
            P(("ga", "aa"), "ba"),
            P(("ga", "aa"), "ba"),
            P(("ga", "aa")),
            P(("ga", "ba"), "aa"),
            P("ba", "aa"),
            P("aa"),
            P("aa", None),
            P(("ga", "ba")),
            P(("ga", "ba")),
            P("ba", None, "aa"),
            P("ba", None, "aa"),
            P("ba", "aa", None),
        ),
        out_specs=P(("ga", "ba"), "aa"),
        check_vma=False,
    )
```

```python
import functools

import jax
import jax.numpy as jnp
from jax import lax
from jax.experimental import pallas as pl
from jax.experimental.pallas import tpu as pltpu
from jax.sharding import PartitionSpec as P

D = 5120
HD = 128
Q = 1024
STEP = 1024
LOADS = 4
PARTS = 4
EARLY = 2
PROJECT_GRANT = 67043328
TILE = 256
EXPERTS_GRANT = 67043328
ATTEND_GRANT = 67043328
LANES = 128
LOG2E = 1.4426950408889634


NEGATIVE = -1e30
EPSILON = 1e-05


def attend_kernel(shards, group, *refs):
    lengths, q_ref, refs = refs[:shards], refs[shards], refs[shards + 1 :]
    sources = refs[: 2 * shards]
    out_ref, stat_ref, kv_ref, stack_ref, peak_ref, acc_ref, sems = refs[2 * shards :]
    factor = HD ** (-0.5) * LOG2E
    rows = q_ref.shape[0]
    context = kv_ref.shape[2]
    step = min(STEP, context)
    tails = [size for size in (step // 2, step) if size % LANES == 0]
    g = pl.program_id(0)
    column = pl.ds(pl.multiple_of(g * HD, HD), HD)

    @pl.when(g == 0)
    def _():
        for at, source in enumerate(sources):
            pltpu.make_async_copy(source, kv_ref.at[at // 2, at % 2], sems.at[at // 2, at % 2]).start()

    for head in range(group):
        stack_ref[head * rows : (head + 1) * rows, :] = q_ref[:, head * HD : (head + 1) * HD]
    peak_ref[...] = jnp.full_like(peak_ref, NEGATIVE)
    acc_ref[...] = jnp.zeros_like(acc_ref)

    def chunk(shard, start, size, limit):
        k = kv_ref[shard, 0, pl.ds(start, size), column]
        v = kv_ref[shard, 1, pl.ds(start, size), column]
        v = jnp.concatenate([v, jnp.ones((size, HD), jnp.bfloat16)], axis=1)
        for head in range(group):
            span = slice(head * rows, (head + 1) * rows)
            scores = lax.dot_general(
                stack_ref[span, :], k, (((1,), (1,)), ((), ())), preferred_element_type=jnp.float32
            )
            if limit is not None:
                place = lax.broadcasted_iota(jnp.int32, scores.shape, 1)
                scores = jnp.where(place < limit, scores, NEGATIVE)
            old = peak_ref[span, :]
            new = jnp.maximum(old, jnp.max(scores, axis=1, keepdims=True))
            probs = jnp.exp2((scores - new[:, :1]) * factor).astype(jnp.bfloat16)
            scale = jnp.exp2((old - new) * factor)
            peak_ref[span, :] = new
            acc_ref[span, :] = acc_ref[span, :] * jnp.concatenate([scale, scale], axis=1) + jnp.dot(
                probs, v, preferred_element_type=jnp.float32
            )

    @pl.loop(0, shards)
    def _(shard):
        @pl.when(g == 0)
        def _():
            for part in range(2):
                pltpu.make_async_copy(
                    sources[part], kv_ref.at[shard, part], sems.at[shard, part]
                ).wait()

        length = lengths[0][0]
        for at in range(1, shards):
            length = jnp.where(shard == at, lengths[at][0], length)
        full = length // step
        left = length - full * step
        start = pl.multiple_of(full * step, step)

        @pl.loop(0, full)
        def _(i):
            chunk(shard, pl.multiple_of(i * step, step), step, None)

        low = 0
        for size in tails:

            @pl.when((left > low) & (left <= size))
            def _(size=size):
                chunk(shard, start, size, left)

            low = size

    for head in range(group):
        span = slice(head * rows, (head + 1) * rows)
        out_ref[:, head * HD : (head + 1) * HD] = (acc_ref[span, :HD] / acc_ref[span, HD:]).astype(
            out_ref.dtype
        )
        stat_ref[0, 0, head : head + 1, :] = jnp.transpose(peak_ref[span, :])[0:1, :]
        stat_ref[0, 1, head : head + 1, :] = jnp.transpose(acc_ref[span, HD:])[0:1, :]


def attend(query, key_blocks, value_blocks, lengths, out_type):
    shards = len(key_blocks)
    rows, width = query.shape
    context, kv_width = key_blocks[0].shape
    kv_heads = kv_width // HD
    group = width // HD // kv_heads
    work = shards * rows * width * context
    sources = [array for pair in zip(key_blocks, value_blocks) for array in pair]
    return pl.pallas_call(
        functools.partial(attend_kernel, shards, group),
        grid_spec=pltpu.PrefetchScalarGridSpec(
            num_scalar_prefetch=shards,
            grid=(kv_heads,),
            in_specs=[pl.BlockSpec((rows, group * HD), lambda g, *n: (0, g))]
            + [pl.BlockSpec(memory_space=pl.ANY)] * (2 * shards),
            out_specs=[
                pl.BlockSpec((rows, group * HD), lambda g, *n: (0, g)),
                pl.BlockSpec((1, 2, group, rows), lambda g, *n: (g, 0, 0, 0)),
            ],
            scratch_shapes=[
                pltpu.VMEM((shards, 2, context, kv_width), jnp.bfloat16),
                pltpu.VMEM((group * rows, HD), jnp.bfloat16),
                pltpu.VMEM((group * rows, HD), jnp.float32),
                pltpu.VMEM((group * rows, 2 * HD), jnp.float32),
                pltpu.SemaphoreType.DMA((shards, 2)),
            ],
        ),
        out_shape=[
            jax.ShapeDtypeStruct((rows, width), out_type),
            jax.ShapeDtypeStruct((kv_heads, 2, group, rows), jnp.float32),
        ],
        cost_estimate=pl.CostEstimate(
            flops=4 * work, bytes_accessed=4 * shards * context * kv_heads * HD + 6 * rows * width,
            transcendentals=work // HD,
        ),
        compiler_params=pltpu.CompilerParams(vmem_limit_bytes=ATTEND_GRANT),
        name="attend",
    )(*lengths, query, *sources)


def span_attention(query, keys, values, cache_lengths):
    size = lax.axis_size("aa")
    swap = [(i, i ^ 1) for i in range(size)]
    far = []
    for hop in range(2, size, 2):
        ahead = [(i, (i + hop) % size) for i in range(size)]
        far.append((lax.ppermute(query, "aa", ahead), [(j, i) for i, j in ahead]))
    near_keys = lax.ppermute(keys, "aa", swap)
    near_values = lax.ppermute(values, "aa", swap)
    near_length = lax.ppermute(cache_lengths, "aa", swap)
    parts = [attend(query, [keys], [values], [cache_lengths], jnp.float32)]
    for rows, back in far:
        rows, parts[0] = lax.optimization_barrier((rows, parts[0]))
        out, stat = attend(
            rows,
            [keys, near_keys],
            [values, near_values],
            [cache_lengths, near_length],
            jnp.bfloat16,
        )
        parts.append((lax.ppermute(out, "aa", back), lax.ppermute(stat, "aa", back)))
    parts.append(attend(query, [near_keys], [near_values], [near_length], jnp.float32))
    return merge(parts, keys.shape[1] // HD)


def merge_kernel(count, group, *refs):
    stats, outs, out_ref = refs[:count], refs[count : 2 * count], refs[-1]
    factor = HD ** (-0.5) * LOG2E
    rows = out_ref.shape[0]
    top = functools.reduce(jnp.maximum, [stat[0, 0] for stat in stats])
    weights = [stat[0, 1] * jnp.exp2((stat[0, 0] - top) * factor) for stat in stats]
    whole = functools.reduce(jnp.add, weights)
    shares = [weight / whole for weight in weights]
    for head in range(group):
        span = slice(head * HD, (head + 1) * HD)
        terms = [
            out[:, span].astype(jnp.float32)
            * jnp.transpose(jnp.broadcast_to(share[head : head + 1, :], (HD, rows)))
            for out, share in zip(outs, shares)
        ]
        out_ref[:, span] = functools.reduce(jnp.add, terms).astype(out_ref.dtype)


def merge(parts, kv_heads):
    count = len(parts)
    rows, width = parts[0][0].shape
    group = width // HD // kv_heads
    wide = pl.BlockSpec((rows, group * HD), lambda g: (0, g))
    return pl.pallas_call(
        functools.partial(merge_kernel, count, group),
        grid=(kv_heads,),
        in_specs=[pl.BlockSpec((1, 2, group, rows), lambda g: (g, 0, 0, 0))] * count + [wide] * count,
        out_specs=wide,
        out_shape=jax.ShapeDtypeStruct((rows, width), jnp.bfloat16),
        compiler_params=pltpu.CompilerParams(vmem_limit_bytes=ATTEND_GRANT),
        name="merge",
    )(*[stat for _, stat in parts], *[out for out, _ in parts])


def peers_of(me_a, me_b, n, m):
    peers = [{"ba": lax.rem(me_b + k, m)} for k in range(1, m)]
    peers += [{"aa": lax.rem(me_a + hop, n)} for hop in range(2, n, 2)]
    return peers + [{"aa": partner_of(me_a)}]


def partner_of(me_a):
    return me_a + 1 - 2 * lax.rem(me_a, 2)


def meet(peers):
    barrier = pltpu.get_barrier_semaphore()
    for peer in peers:
        pl.semaphore_signal(barrier, inc=1, device_id=peer, device_id_type=pl.DeviceIdType.MESH)
    pl.semaphore_wait(barrier, len(peers))


def remote(source, target, send, receive, peer):
    copy = pltpu.make_async_remote_copy(
        src_ref=source,
        dst_ref=target,
        send_sem=send,
        recv_sem=receive,
        device_id=peer,
        device_id_type=pl.DeviceIdType.MESH,
    )
    copy.start()
    return copy


def dispatch_kernel(local, n, m, packed, out, own_sem, z_send, z_recv, x_send, x_recv, c_send, c_recv):
    me_a, me_b = lax.axis_index("aa"), lax.axis_index("ba")
    slots, columns = packed.shape[1], packed.shape[2]
    meet(peers_of(me_a, me_b, n, 1 if local else m))

    def index(k):
        return k if local else lax.rem(me_b - k + m, m)

    def place(b, a):
        if len(out.shape) == 3:
            return out.at[a, pl.ds(pl.multiple_of(b * slots, slots), slots)]
        return out.at[
            pl.ds(pl.multiple_of(b * slots, slots), slots),
            pl.ds(pl.multiple_of(a * columns, columns), columns),
        ]

    own = []
    for k in range(m if local else 1):
        own.append(pltpu.make_async_copy(packed.at[index(k)], place(index(k), me_a), own_sem.at[k]))
        own[k].start()
    over_z = [None]
    for k in range(1, 1 if local else m):
        to = lax.rem(me_b + k, m)
        over_z.append(
            remote(packed.at[to], place(me_b, me_a), z_send.at[k], z_recv.at[k], {"ba": to})
        )
    partner = partner_of(me_a)
    over_x, over_c = {}, {}

    def forward(k):
        b = index(k)
        for j, hop in enumerate(range(2, n, 2), 1):
            over_x[k, j].wait_recv()
            block = place(b, lax.rem(me_a - hop + n, n))
            over_c[k, j] = remote(
                block, block, c_send.at[k, j], c_recv.at[k, j], {"aa": partner}
            )

    for k in range(m):
        if k < len(own):
            own[k].wait()
        else:
            over_z[k].wait_recv()
        block = place(index(k), me_a)
        for j, hop in enumerate(range(2, n, 2), 1):
            over_x[k, j] = remote(
                block,
                block,
                x_send.at[k, j],
                x_recv.at[k, j],
                {"aa": lax.rem(me_a + hop, n)},
            )
        over_c[k, 0] = remote(block, block, c_send.at[k, 0], c_recv.at[k, 0], {"aa": partner})
        if k > 0:
            forward(k - 1)
    forward(m - 1)
    for copy in over_c.values():
        copy.wait_recv()
    for copy in over_z[1:] + list(over_x.values()) + list(over_c.values()):
        copy.wait_send()


def dispatch(packed, local, m, name, number):
    n = lax.axis_size("aa")
    columns = packed.shape[1]
    rows = packed.shape[0] // m
    half = n // 2
    sems = [pltpu.SemaphoreType.DMA((m,))] * 2 + [pltpu.SemaphoreType.DMA((m, half))] * 4
    flat = columns % LANES == 0 and not local
    shape = (m * rows, n * columns) if flat else (n, m * rows, columns)
    out = pl.pallas_call(
        functools.partial(dispatch_kernel, local, n, m),
        out_shape=jax.ShapeDtypeStruct(shape, packed.dtype),
        in_specs=[pl.BlockSpec(memory_space=pltpu.VMEM)],
        out_specs=pl.BlockSpec(memory_space=pltpu.VMEM),
        scratch_shapes=[pltpu.SemaphoreType.DMA((m,))] + sems,
        compiler_params=pltpu.CompilerParams(
            collective_id=number, has_side_effects=True, vmem_limit_bytes=24 * 1024 * 1024
        ),
        name=name,
    )(packed.reshape(m, rows, columns))
    if local:
        return out.reshape(n * m * rows, columns)
    return out if flat else out.transpose(1, 0, 2).reshape(m * rows, n * columns)


def combine_kernel(
    n, m, part, out, near, summed, far, total, own_sem, z_send, z_recv, x_send, x_recv, c_send, c_recv
):
    me_a, me_b = lax.axis_index("aa"), lax.axis_index("ba")
    slots, columns = out.shape[1], out.shape[2]
    meet(peers_of(me_a, me_b, n, m))
    partner = partner_of(me_a)

    def piece(k, a):
        b = lax.rem(me_b + k, m)
        if len(part.shape) == 3:
            return part.at[a, pl.ds(pl.multiple_of(b * slots, slots), slots)]
        return part.at[
            pl.ds(pl.multiple_of(b * slots, slots), slots),
            pl.ds(pl.multiple_of(a * columns, columns), columns),
        ]

    order = list(range(1, m)) + [0]
    over_c, over_x = {}, {}
    over_z = [None] * m
    for k in order:
        for j in range(n // 2):
            over_c[k, j] = remote(
                piece(k, lax.rem(partner + 2 * j, n)),
                near.at[k, j],
                c_send.at[k, j],
                c_recv.at[k, j],
                {"aa": partner},
            )

    def join(k, j):
        over_c[k, j].wait_recv()
        mine = piece(k, lax.rem(me_a + 2 * j, n))
        return mine[...].astype(jnp.float32) + near[k, j].astype(jnp.float32)

    def finish(k):
        value = join(k, 0)
        for j in range(1, n // 2):
            over_x[k, j].wait_recv()
            value = value + far[k, j].astype(jnp.float32)
        total[k] = value.astype(total.dtype)
        if k == 0:
            copy = pltpu.make_async_copy(total.at[0], out.at[me_b], own_sem)
            copy.start()
            copy.wait()
        else:
            over_z[k] = remote(
                total.at[k],
                out.at[me_b],
                z_send.at[k],
                z_recv.at[k],
                {"ba": lax.rem(me_b + k, m)},
            )

    for k in order:
        for j in range(1, n // 2):
            summed[k, j] = join(k, j).astype(summed.dtype)
            over_x[k, j] = remote(
                summed.at[k, j],
                far.at[k, j],
                x_send.at[k, j],
                x_recv.at[k, j],
                {"aa": lax.rem(me_a + 2 * j, n)},
            )
    for k in order:
        finish(k)
    for copy in over_z[1:]:
        copy.wait_recv()
    for copy in over_z[1:] + list(over_x.values()) + list(over_c.values()):
        copy.wait_send()


def combine(part):
    n, m = lax.axis_size("aa"), lax.axis_size("ba")
    rows, columns = part.shape[0] // m, part.shape[1] // n
    if columns % LANES:
        part = part.reshape(m * rows, n, columns).transpose(1, 0, 2)
    half = n // 2
    sems = [pltpu.SemaphoreType.DMA((m,))] * 2 + [pltpu.SemaphoreType.DMA((m, half))] * 4
    block = pltpu.VMEM((m, half, rows, columns), part.dtype)
    out = pl.pallas_call(
        functools.partial(combine_kernel, n, m),
        out_shape=jax.ShapeDtypeStruct((m, rows, columns), part.dtype),
        in_specs=[pl.BlockSpec(memory_space=pltpu.VMEM)],
        out_specs=pl.BlockSpec(memory_space=pltpu.VMEM),
        scratch_shapes=[block, block, block, pltpu.VMEM((m, rows, columns), part.dtype)]
        + [pltpu.SemaphoreType.DMA]
        + sems,
        compiler_params=pltpu.CompilerParams(
            collective_id=2, has_side_effects=True, vmem_limit_bytes=40 * 1024 * 1024
        ),
        name="combine",
    )(part)
    return out.reshape(m * rows, columns)


def experts_kernel(
    n,
    m,
    packed,
    gate_hbm,
    up_hbm,
    down_hbm,
    out,
    inputs,
    gate_w,
    up_w,
    down_w,
    sums,
    act,
    part,
    near,
    summed,
    far,
    total,
    load_sem,
    own_sem,
    z_send,
    z_recv,
    x_send,
    x_recv,
    c_send,
    c_recv,
    f_send,
    f_recv,
    bz_send,
    bz_recv,
    bx_send,
    bx_recv,
    bc_send,
    bc_recv,
):
    me_a, me_b = lax.axis_index("aa"), lax.axis_index("ba")
    slots, columns = packed.shape[1], packed.shape[2]
    width = n * columns
    hidden = gate_w.shape[1]
    across, partner = flip(me_a, 2), flip(me_a, 1)
    order = [0, 2, 1, 3]
    block_of = [flip(me_b, way) for way in order]

    loads = []
    for at, (source, target) in enumerate(
        ((gate_hbm, gate_w), (up_hbm, up_w), (down_hbm, down_w))
    ):
        piece = target.shape[0] // LOADS
        for i in range(LOADS):
            rows = pl.ds(i * piece, piece)
            loads.append(
                pltpu.make_async_copy(source.at[0, rows], target.at[rows], load_sem.at[at, i])
            )
            loads[-1].start()
    meet([{"ba": block_of[k]} for k in range(1, m)] + [{"aa": across}, {"aa": partner}])

    def place(k, a):
        return inputs.at[
            k * slots : (k + 1) * slots, pl.ds(pl.multiple_of(a * columns, columns), columns)
        ]

    over_z, over_x, over_c, over_f = {}, {}, {}, {}
    own = pltpu.make_async_copy(packed.at[me_b], place(0, me_a), own_sem)
    for k in range(1, m):
        over_z[k] = remote(
            packed.at[block_of[k]], place(k, me_a), z_send.at[k], z_recv.at[k], {"ba": block_of[k]}
        )

    def spread(k):
        if k:
            over_z[k].wait_recv()
        block = place(k, me_a)
        source = block if k else packed.at[me_b]
        over_x[k] = remote(source, block, x_send.at[k], x_recv.at[k], {"aa": across})
        over_c[k] = remote(source, block, c_send.at[k], c_recv.at[k], {"aa": partner})

    def forward(k):
        over_x[k].wait_recv()
        block = place(k, across)
        over_f[k] = remote(block, block, f_send.at[k], f_recv.at[k], {"aa": partner})

    def dots(pair, half, side, finish):
        rows = slice(2 * pair * slots, 2 * (pair + 1) * slots)
        if side is None:
            deep = slice(0, width)
        else:
            deep = pl.ds(pl.multiple_of(side * (width // 2), width // 2), width // 2)

        @pl.loop(0, hidden // 2 // TILE)
        def _(i):
            span = pl.ds(pl.multiple_of(half * (hidden // 2) + i * TILE, TILE), TILE)
            x = inputs[rows, deep]
            gate = jnp.dot(x, gate_w[deep, span], preferred_element_type=jnp.float32)
            up = jnp.dot(x, up_w[deep, span], preferred_element_type=jnp.float32)
            if not finish:
                sums[0, :, span] = gate
                sums[1, :, span] = up
                return
            if side is not None:
                gate = gate + sums[0, :, span]
                up = up + sums[1, :, span]
            act[rows, span] = (jax.nn.silu(gate) * up).astype(jnp.bfloat16)

    back_c, back_x, back_z = {}, {}, {}

    def lower(pair, a):
        rows = slice(2 * pair * slots, 2 * (pair + 1) * slots)

        @pl.loop(0, columns // TILE)
        def _(i):
            span = pl.ds(pl.multiple_of(a * columns + i * TILE, TILE), TILE)
            part[rows, span] = jnp.dot(
                act[rows, :], down_w[:, span], preferred_element_type=jnp.float32
            ).astype(jnp.bfloat16)

    def piece(k, a):
        return part.at[
            k * slots : (k + 1) * slots, pl.ds(pl.multiple_of(a * columns, columns), columns)
        ]

    def hand(k, j, a):
        back_c[k, j] = remote(
            piece(k, a), near.at[k, j], bc_send.at[k, j], bc_recv.at[k, j], {"aa": partner}
        )

    def join(k, j, a):
        back_c[k, j].wait_recv()
        return piece(k, a)[...].astype(jnp.float32) + near[k, j].astype(jnp.float32)

    def cross(k):
        summed[k] = join(k, 1, across).astype(summed.dtype)
        back_x[k] = remote(
            summed.at[k], far.at[k], bx_send.at[k], bx_recv.at[k], {"aa": across}
        )

    def finish(k):
        value = join(k, 0, me_a)
        back_x[k].wait_recv()
        value = value + far[k].astype(jnp.float32)
        if k == 0:
            out[me_b] = value.astype(out.dtype)
        else:
            total[k] = value.astype(total.dtype)
            back_z[k] = remote(
                total.at[k], out.at[me_b], bz_send.at[k], bz_recv.at[k], {"ba": block_of[k]}
            )

    def descend(pair):
        first, second = 2 * pair + 1, 2 * pair
        lower(pair, flip(partner, 2))
        hand(first, 1, flip(partner, 2))
        hand(second, 1, flip(partner, 2))
        lower(pair, across)
        cross(first)
        cross(second)
        lower(pair, partner)
        hand(first, 0, partner)
        hand(second, 0, partner)
        lower(pair, me_a)

    spread(0)
    own.start()
    forward(0)
    spread(1)
    for copy in loads[: 2 * LOADS]:
        copy.wait()
    own.wait()
    over_c[0].wait_recv()
    over_c[1].wait_recv()
    side = me_a // 2
    dots(0, 0, side, False)
    dots(0, 1, side, False)
    spread(2)
    forward(1)
    over_f[0].wait_recv()
    over_f[1].wait_recv()
    dots(0, 0, 1 - side, True)
    dots(0, 1, 1 - side, True)
    spread(3)
    forward(2)
    for copy in loads[2 * LOADS :]:
        copy.wait()
    descend(0)
    forward(3)
    for k in (2, 3):
        over_c[k].wait_recv()
        over_f[k].wait_recv()
    dots(1, 0, None, True)
    finish(1)
    dots(1, 1, None, True)
    finish(0)
    descend(1)
    finish(3)
    finish(2)
    for copy in back_z.values():
        copy.wait_recv()
    for group in (over_z, over_x, over_c, over_f, back_c, back_x, back_z):
        for copy in group.values():
            copy.wait_send()


def flip(index, way):
    for bit in (1, 2):
        if way & bit:
            index = index + bit - 2 * bit * lax.rem(index // bit, 2)
    return index


def run_experts(packed, gate_w, up_w, down_w):
    n, m = lax.axis_size("aa"), lax.axis_size("ba")
    rows, columns = packed.shape[1:]
    depth, hidden = gate_w.shape[1:]
    block = pltpu.VMEM((m, rows, columns), jnp.bfloat16)
    one, two = pltpu.SemaphoreType.DMA((m,)), pltpu.SemaphoreType.DMA((m, 2))
    out = pl.pallas_call(
        functools.partial(experts_kernel, n, m),
        out_shape=jax.ShapeDtypeStruct((m, rows, columns), jnp.bfloat16),
        in_specs=[pl.BlockSpec(memory_space=pl.ANY)] * 4,
        out_specs=pl.BlockSpec(memory_space=pltpu.VMEM),
        scratch_shapes=[
            pltpu.VMEM((m * rows, n * columns), jnp.bfloat16),
            pltpu.VMEM((depth, hidden), jnp.bfloat16),
            pltpu.VMEM((depth, hidden), jnp.bfloat16),
            pltpu.VMEM((hidden, n * columns), jnp.bfloat16),
            pltpu.VMEM((2, 2 * rows, hidden), jnp.float32),
            pltpu.VMEM((m * rows, hidden), jnp.bfloat16),
            pltpu.VMEM((m * rows, n * columns), jnp.bfloat16),
            pltpu.VMEM((m, 2, rows, columns), jnp.bfloat16),
            block,
            block,
            block,
            pltpu.SemaphoreType.DMA((3, LOADS)),
            pltpu.SemaphoreType.DMA,
        ]
        + [one] * 12
        + [two] * 2,
        compiler_params=pltpu.CompilerParams(
            collective_id=1, has_side_effects=True, vmem_limit_bytes=EXPERTS_GRANT
        ),
        name="experts",
    )(packed, gate_w, up_w, down_w)
    return out.reshape(m * rows, columns)


def plain_experts(packed, gate_w, up_w, down_w):
    piece = dispatch(packed, False, lax.axis_size("ba"), "dispatch", 1)
    gate_part = jnp.dot(piece, gate_w, preferred_element_type=jnp.float32)
    up_part = jnp.dot(piece, up_w, preferred_element_type=jnp.float32)
    act = (jax.nn.silu(gate_part) * up_part).astype(jnp.bfloat16)
    return combine(jnp.dot(act, down_w, preferred_element_type=jnp.float32).astype(jnp.bfloat16))


def project_kernel(
    n,
    m,
    own,
    weight_hbm,
    residual_hbm,
    gain,
    router,
    ids,
    places,
    hidden_hbm,
    packed_hbm,
    gate_hbm,
    hidden,
    packed,
    gate,
    rows_in,
    weight,
    residual,
    up,
    down,
    leaving,
    value,
    stats,
    normed,
    mix,
    placing,
    load_sem,
    store_sem,
    x_send,
    x_recv,
    c_send,
    c_recv,
    f_send,
    f_recv,
    u_send,
    u_recv,
    d_send,
    d_recv,
    s_send,
    s_recv,
):
    me_a, me_b = lax.axis_index("aa"), lax.axis_index("ba")
    rows, columns = hidden.shape
    experts = router.shape[0]
    slots = packed.shape[1]
    part = rows // PARTS
    across, partner = flip(me_a, 2), flip(me_a, 1)
    loads = [
        pltpu.make_async_copy(weight_hbm, weight, load_sem.at[0]),
        pltpu.make_async_copy(residual_hbm, residual, load_sem.at[1]),
        pltpu.make_async_copy(own, rows_in.at[0], load_sem.at[2]),
    ]
    for copy in loads:
        copy.start()
    meet(
        [{"ba": lax.rem(me_b + k, m)} for k in range(1, m)]
        + [{"aa": flip(me_a, way)} for way in range(1, n)]
    )

    def cut(c):
        return pl.ds(pl.multiple_of(c * part, part), part)

    def pass_on(slot, target, sends, receives, peer, c):
        return pltpu.make_async_remote_copy(
            src_ref=(own if target < 3 else rows_in.at[slot]).at[cut(c)],
            dst_ref=rows_in.at[target, cut(c)],
            send_sem=sends.at[c],
            recv_sem=receives.at[c],
            device_id={"aa": peer},
            device_id_type=pl.DeviceIdType.MESH,
        )

    over_x = functools.partial(pass_on, 0, 2, x_send, x_recv, across)
    over_c = functools.partial(pass_on, 0, 1, c_send, c_recv, partner)
    over_f = functools.partial(pass_on, 2, 3, f_send, f_recv, partner)
    for c in range(PARTS):
        over_x(c).start()
    for c in range(PARTS):
        over_c(c).start()
    half, low = me_b // 2, lax.rem(me_b, 2)
    order = [3 - 3 * half, 2 - half, 2 * half + 1 - low, me_b]

    def climb(b, c, target):
        return pltpu.make_async_remote_copy(
            src_ref=leaving.at[b, cut(c)],
            dst_ref=up.at[b, cut(c)],
            send_sem=u_send.at[b, c],
            recv_sem=u_recv.at[b, c],
            device_id={"ba": target},
            device_id_type=pl.DeviceIdType.MESH,
        )

    def sink(b, c, target):
        return pltpu.make_async_remote_copy(
            src_ref=leaving.at[b, cut(c)],
            dst_ref=down.at[b, cut(c)],
            send_sem=d_send.at[b, c],
            recv_sem=d_recv.at[b, c],
            device_id={"ba": target},
            device_id_type=pl.DeviceIdType.MESH,
        )

    above, below = lax.rem(me_b + 1, m), lax.rem(me_b + m - 1, m)
    for copy in (loads[2], loads[0]):
        copy.wait()

    def step(at, c):
        b = order[at]
        slot = lax.rem(b // 2 + me_a // 2, 2) * 2 + lax.rem(b + me_a, 2)
        value[...] = jnp.dot(
            rows_in[slot, cut(c), :], weight[...], preferred_element_type=jnp.float32
        )

        @pl.when((b >= me_b) & (me_b > 0))
        def _():
            climb(b, c, above).wait_recv()
            value[...] += up[b, cut(c), :].astype(jnp.float32)

        @pl.when((b <= me_b) & (me_b < m - 1))
        def _():
            sink(b, c, below).wait_recv()
            value[...] += down[b, cut(c), :].astype(jnp.float32)

        if at == m - 1:
            hidden[cut(c), :] = residual[cut(c), :].astype(jnp.float32) + value[...]
            return
        leaving[b, cut(c), :] = value[...].astype(leaving.dtype)

        @pl.when(b > me_b)
        def _():
            climb(b, c, above).start()

        @pl.when(b < me_b)
        def _():
            sink(b, c, below).start()

    place = jnp.where(places[...] >= 0, ids[...] * slots + places[...], -1)
    placing[...] = (
        lax.broadcasted_iota(jnp.int32, placing.shape, 0) == place
    ).astype(jnp.bfloat16)
    for c in range(PARTS):
        over_c(c).wait_recv()
    edge = (me_b == 0) | (me_b == m - 1)
    early = edge & (order[0] // 2 != me_a // 2)

    @pl.when(early)
    def _():
        @pl.loop(0, EARLY)
        def _(c):
            step(2, c)

    @pl.loop(0, PARTS)
    def _(c):
        over_x(c).wait_recv()
        over_f(c).start()
        over_f(c).wait_recv()
        step(0, c)

    @pl.loop(0, PARTS)
    def _(c):
        step(1, c)

        @pl.when((early & (c < EARLY)) == False)
        def _():
            step(2, c)

    loads[1].wait()

    @pl.loop(0, PARTS)
    def _(c):
        step(3, c)
        kept = hidden[cut(c), :]
        lane = lax.broadcasted_iota(jnp.int32, (part, LANES), 1)
        square = jnp.sum(kept * kept, axis=1, keepdims=True)
        found = jnp.where(lane == experts, square, 0.0)
        scaled = kept * gain[...]
        for e in range(experts):
            logit = jnp.sum(scaled * router[e : e + 1, :], axis=1, keepdims=True)
            found = jnp.where(lane == e, logit, found)
        mix[cut(c), :] = found

    stores = [pltpu.make_async_copy(hidden, hidden_hbm, store_sem.at[m])]
    stores[0].start()
    stats[0] = jnp.transpose(mix[...])[: stats.shape[1], :]
    over_s = [
        remote(
            stats.at[0],
            stats.at[way],
            s_send.at[way],
            s_recv.at[way],
            {"aa": flip(me_a, way)},
        )
        for way in range(1, n)
    ]
    for copy in over_s:
        copy.wait_recv()
    sums = functools.reduce(jnp.add, [stats[way] for way in range(n)])
    inverse = 1.0 / jnp.sqrt(sums[experts : experts + 1, :] / (n * columns) + EPSILON)
    chosen = ids[...] == lax.broadcasted_iota(jnp.int32, (experts, rows), 0)
    gate[...] = jnp.sum(
        jnp.where(chosen, jax.nn.sigmoid(sums[:experts, :] * inverse), 0.0), axis=0, keepdims=True
    )
    stores.append(pltpu.make_async_copy(gate, gate_hbm, store_sem.at[m + 1]))
    stores[-1].start()
    spread = jnp.transpose(jnp.broadcast_to(inverse, (LANES, rows)))
    for at in range(0, columns, LANES):
        span = slice(at, at + LANES)
        normed[:, span] = (hidden[:, span] * spread * gain[:, span]).astype(jnp.bfloat16)
    for b in range(m):
        packed[b] = jnp.dot(
            placing[b * slots : (b + 1) * slots, :],
            normed[...],
            preferred_element_type=jnp.float32,
        ).astype(packed.dtype)
        stores.append(pltpu.make_async_copy(packed.at[b], packed_hbm.at[b], store_sem.at[b]))
        stores[-1].start()
    for copy in over_s:
        copy.wait_send()

    @pl.loop(0, PARTS)
    def _(c):
        for copy in (over_x, over_c, over_f):
            copy(c).wait_send()
        for at in range(m - 1):

            @pl.when(order[at] > me_b)
            def _(b=order[at], c=c):
                climb(b, c, above).wait_send()

            @pl.when(order[at] < me_b)
            def _(b=order[at], c=c):
                sink(b, c, below).wait_send()

    for copy in stores:
        copy.wait()


def project(own, weight, residual, gain, router, ids, places):
    n, m = lax.axis_size("aa"), lax.axis_size("ba")
    rows, columns = residual.shape
    experts = router.shape[1]
    slots = 2 * rows // experts
    block = pltpu.VMEM((m, rows, columns), jnp.bfloat16)
    one, two = pltpu.SemaphoreType.DMA((PARTS,)), pltpu.SemaphoreType.DMA((m, PARTS))
    vmem, anywhere = pl.BlockSpec(memory_space=pltpu.VMEM), pl.BlockSpec(memory_space=pl.ANY)
    return pl.pallas_call(
        functools.partial(project_kernel, n, m),
        out_shape=[
            jax.ShapeDtypeStruct((rows, columns), jnp.float32),
            jax.ShapeDtypeStruct((m, slots, columns), jnp.bfloat16),
            jax.ShapeDtypeStruct((1, rows), jnp.float32),
        ],
        in_specs=[anywhere, anywhere, anywhere, vmem, vmem, vmem, vmem],
        out_specs=[anywhere] * 3,
        scratch_shapes=[
            pltpu.VMEM((rows, columns), jnp.float32),
            pltpu.VMEM((m, slots, columns), jnp.bfloat16),
            pltpu.VMEM((1, rows), jnp.float32),
            pltpu.VMEM((n, rows, own.shape[1]), jnp.bfloat16),
            pltpu.VMEM(weight.shape, jnp.bfloat16),
            pltpu.VMEM((rows, columns), jnp.bfloat16),
            block,
            block,
            block,
            pltpu.VMEM((rows // PARTS, columns), jnp.float32),
            pltpu.VMEM((n, 8, rows), jnp.float32),
            pltpu.VMEM((rows, columns), jnp.bfloat16),
            pltpu.VMEM((rows, LANES), jnp.float32),
            pltpu.VMEM((m * slots, rows), jnp.bfloat16),
            pltpu.SemaphoreType.DMA((3,)),
            pltpu.SemaphoreType.DMA((m + 2,)),
        ]
        + [one] * 6
        + [two] * 4
        + [pltpu.SemaphoreType.DMA((n,))] * 2,
        compiler_params=pltpu.CompilerParams(
            collective_id=4, has_side_effects=True, vmem_limit_bytes=PROJECT_GRANT
        ),
        name="project",
    )(
        own,
        weight,
        residual,
        gain.reshape(1, columns),
        router.T,
        ids.reshape(1, rows),
        places.reshape(1, rows),
    )


def placing_of(expert_ids, expert_slots, experts):
    slot_count = 2 * expert_ids.shape[0] // experts
    combined = expert_ids * slot_count + expert_slots
    placing = (
        combined[:, None] == lax.broadcasted_iota(jnp.int32, (1, experts * slot_count), 1)
    ) & (expert_slots[:, None] >= 0)
    return placing.astype(jnp.bfloat16)


def plain_project(
    own, out_weight, residual, norm_gain, router_weight, expert_ids, expert_slots
):
    attended = dispatch(own, True, 4 if own.shape[0] % 64 == 0 else 1, "gather", 3)
    hidden = residual.astype(jnp.float32) + lax.psum_scatter(
        jnp.dot(attended, out_weight, preferred_element_type=jnp.float32).astype(jnp.bfloat16),
        "ba",
        scatter_dimension=0,
        tiled=True,
    ).astype(jnp.float32)
    scaled = hidden * norm_gain
    sums = lax.psum(
        jnp.concatenate(
            [
                jnp.dot(scaled, router_weight, precision=lax.Precision.HIGHEST),
                jnp.sum(hidden * hidden, axis=1, keepdims=True),
            ],
            axis=1,
        ),
        "aa",
    )
    inverse = 1.0 / jnp.sqrt(sums[:, -1] / D + EPSILON)
    normed = scaled * inverse[:, None]
    logits = sums[:, :-1] * inverse[:, None]
    experts = router_weight.shape[1]
    chosen = expert_ids[:, None] == lax.broadcasted_iota(jnp.int32, (1, experts), 1)
    gate = jnp.sum(jnp.where(chosen, jax.nn.sigmoid(logits), 0.0), axis=1)
    expert_in = normed.astype(jnp.bfloat16)
    placing = placing_of(expert_ids, expert_slots, experts)
    packed = lax.dot_general(
        placing, expert_in, (((0,), (0,)), ((), ())), preferred_element_type=jnp.float32
    ).astype(jnp.bfloat16)
    return hidden, packed, gate


def on_device(
    query,
    keys,
    values,
    cache_lengths,
    residual,
    out_weight,
    norm_gain,
    router_weight,
    expert_ids,
    expert_slots,
    expert_gate,
    expert_up,
    expert_down,
):
    own = span_attention(query, keys, values, cache_lengths)
    n, m = lax.axis_size("aa"), lax.axis_size("ba")
    experts = router_weight.shape[1]
    rows, columns = residual.shape
    if n == 4 and m == 4 and experts == m and own.shape[0] == rows and columns % LANES == 0:
        hidden, packed, gate = project(
            own, out_weight, residual, norm_gain, router_weight, expert_ids, expert_slots
        )
        returned = run_experts(packed, expert_gate, expert_up, expert_down)
        gate = gate[0]
    else:
        hidden, packed, gate = plain_project(
            own, out_weight, residual, norm_gain, router_weight, expert_ids, expert_slots
        )
        returned = plain_experts(packed, expert_gate[0], expert_up[0], expert_down[0])
    placing = placing_of(expert_ids, expert_slots, experts)
    from_experts = jnp.dot(placing, returned, preferred_element_type=jnp.float32)
    return (hidden + gate[:, None] * from_experts).astype(jnp.bfloat16)


def solution(mesh):
    return jax.shard_map(
        on_device,
        mesh=mesh,
        in_specs=(
            P(("ga", "aa"), "ba"),
            P(("ga", "aa"), "ba"),
            P(("ga", "aa"), "ba"),
            P(("ga", "aa")),
            P(("ga", "ba"), "aa"),
            P("ba", "aa"),
            P("aa"),
            P("aa", None),
            P(("ga", "ba")),
            P(("ga", "ba")),
            P("ba", None, "aa"),
            P("ba", None, "aa"),
            P("ba", "aa", None),
        ),
        out_specs=P(("ga", "ba"), "aa"),
        check_vma=False,
    )
```

```python
import functools

import jax
import jax.numpy as jnp
from jax import lax
from jax.experimental import pallas as pl
from jax.experimental.pallas import tpu as pltpu
from jax.sharding import PartitionSpec as P

D = 5120
HD = 128
Q = 1024
STEP = 1024
LOADS = 4
PARTS = 4
EARLY = 2
PROJECT_GRANT = 67043328
TILE = 256
EXPERTS_GRANT = 67043328
ATTEND_GRANT = 67043328
LANES = 128
LOG2E = 1.4426950408889634


NEGATIVE = -1e30
EPSILON = 1e-05


def attend_kernel(shards, group, *refs):
    lengths, q_ref, refs = refs[:shards], refs[shards], refs[shards + 1 :]
    sources = refs[: 2 * shards]
    out_ref, stat_ref, kv_ref, stack_ref, peak_ref, acc_ref, sems = refs[2 * shards :]
    factor = HD ** (-0.5) * LOG2E
    rows = q_ref.shape[0]
    context = kv_ref.shape[2]
    step = min(STEP, context)
    tails = [size for size in (step // 4, step // 2, step) if size % LANES == 0]
    g = pl.program_id(0)
    column = pl.ds(pl.multiple_of(g * HD, HD), HD)

    @pl.when(g == 0)
    def _():
        for at, source in enumerate(sources):
            pltpu.make_async_copy(source, kv_ref.at[at // 2, at % 2], sems.at[at // 2, at % 2]).start()

    for head in range(group):
        stack_ref[head * rows : (head + 1) * rows, :] = q_ref[:, head * HD : (head + 1) * HD]
    peak_ref[...] = jnp.full_like(peak_ref, NEGATIVE)
    acc_ref[...] = jnp.zeros_like(acc_ref)

    def chunk(shard, start, size, limit):
        k = kv_ref[shard, 0, pl.ds(start, size), column]
        v = kv_ref[shard, 1, pl.ds(start, size), column]
        v = jnp.concatenate([v, jnp.ones((size, HD), jnp.bfloat16)], axis=1)
        for head in range(group):
            span = slice(head * rows, (head + 1) * rows)
            scores = lax.dot_general(
                stack_ref[span, :], k, (((1,), (1,)), ((), ())), preferred_element_type=jnp.float32
            )
            if limit is not None:
                place = lax.broadcasted_iota(jnp.int32, scores.shape, 1)
                scores = jnp.where(place < limit, scores, NEGATIVE)
            old = peak_ref[span, :]
            new = jnp.maximum(old, jnp.max(scores, axis=1, keepdims=True))
            probs = jnp.exp2((scores - new[:, :1]) * factor).astype(jnp.bfloat16)
            scale = jnp.exp2((old - new) * factor)
            peak_ref[span, :] = new
            acc_ref[span, :] = acc_ref[span, :] * jnp.concatenate([scale, scale], axis=1) + jnp.dot(
                probs, v, preferred_element_type=jnp.float32
            )

    @pl.loop(0, shards)
    def _(shard):
        @pl.when(g == 0)
        def _():
            for part in range(2):
                pltpu.make_async_copy(
                    sources[part], kv_ref.at[shard, part], sems.at[shard, part]
                ).wait()

        length = lengths[0][0]
        for at in range(1, shards):
            length = jnp.where(shard == at, lengths[at][0], length)
        full = length // step
        left = length - full * step
        start = pl.multiple_of(full * step, step)

        @pl.loop(0, full)
        def _(i):
            chunk(shard, pl.multiple_of(i * step, step), step, None)

        low = 0
        for size in tails:

            @pl.when((left > low) & (left <= size))
            def _(size=size):
                chunk(shard, start, size, left)

            low = size

    for head in range(group):
        span = slice(head * rows, (head + 1) * rows)
        out_ref[:, head * HD : (head + 1) * HD] = (acc_ref[span, :HD] / acc_ref[span, HD:]).astype(
            out_ref.dtype
        )
        stat_ref[0, 0, head : head + 1, :] = jnp.transpose(peak_ref[span, :])[0:1, :]
        stat_ref[0, 1, head : head + 1, :] = jnp.transpose(acc_ref[span, HD:])[0:1, :]


def attend(query, key_blocks, value_blocks, lengths, out_type):
    shards = len(key_blocks)
    rows, width = query.shape
    context, kv_width = key_blocks[0].shape
    kv_heads = kv_width // HD
    group = width // HD // kv_heads
    work = shards * rows * width * context
    sources = [array for pair in zip(key_blocks, value_blocks) for array in pair]
    return pl.pallas_call(
        functools.partial(attend_kernel, shards, group),
        grid_spec=pltpu.PrefetchScalarGridSpec(
            num_scalar_prefetch=shards,
            grid=(kv_heads,),
            in_specs=[pl.BlockSpec((rows, group * HD), lambda g, *n: (0, g))]
            + [pl.BlockSpec(memory_space=pl.ANY)] * (2 * shards),
            out_specs=[
                pl.BlockSpec((rows, group * HD), lambda g, *n: (0, g)),
                pl.BlockSpec((1, 2, group, rows), lambda g, *n: (g, 0, 0, 0)),
            ],
            scratch_shapes=[
                pltpu.VMEM((shards, 2, context, kv_width), jnp.bfloat16),
                pltpu.VMEM((group * rows, HD), jnp.bfloat16),
                pltpu.VMEM((group * rows, HD), jnp.float32),
                pltpu.VMEM((group * rows, 2 * HD), jnp.float32),
                pltpu.SemaphoreType.DMA((shards, 2)),
            ],
        ),
        out_shape=[
            jax.ShapeDtypeStruct((rows, width), out_type),
            jax.ShapeDtypeStruct((kv_heads, 2, group, rows), jnp.float32),
        ],
        cost_estimate=pl.CostEstimate(
            flops=4 * work, bytes_accessed=4 * shards * context * kv_heads * HD + 6 * rows * width,
            transcendentals=work // HD,
        ),
        compiler_params=pltpu.CompilerParams(vmem_limit_bytes=ATTEND_GRANT),
        name="attend",
    )(*lengths, query, *sources)


def span_attention(query, keys, values, cache_lengths):
    size = lax.axis_size("aa")
    swap = [(i, i ^ 1) for i in range(size)]
    far = []
    for hop in range(2, size, 2):
        ahead = [(i, (i + hop) % size) for i in range(size)]
        far.append((lax.ppermute(query, "aa", ahead), [(j, i) for i, j in ahead]))
    near_keys = lax.ppermute(keys, "aa", swap)
    near_values = lax.ppermute(values, "aa", swap)
    near_length = lax.ppermute(cache_lengths, "aa", swap)
    parts = [attend(query, [keys], [values], [cache_lengths], jnp.float32)]
    for rows, back in far:
        rows, parts[0] = lax.optimization_barrier((rows, parts[0]))
        out, stat = attend(
            rows,
            [keys, near_keys],
            [values, near_values],
            [cache_lengths, near_length],
            jnp.bfloat16,
        )
        parts.append((lax.ppermute(out, "aa", back), lax.ppermute(stat, "aa", back)))
    parts.append(attend(query, [near_keys], [near_values], [near_length], jnp.float32))
    return merge(parts, keys.shape[1] // HD)


def merge_kernel(count, group, *refs):
    stats, outs, out_ref = refs[:count], refs[count : 2 * count], refs[-1]
    factor = HD ** (-0.5) * LOG2E
    rows = out_ref.shape[0]
    top = functools.reduce(jnp.maximum, [stat[0, 0] for stat in stats])
    weights = [stat[0, 1] * jnp.exp2((stat[0, 0] - top) * factor) for stat in stats]
    whole = functools.reduce(jnp.add, weights)
    shares = [weight / whole for weight in weights]
    for head in range(group):
        span = slice(head * HD, (head + 1) * HD)
        terms = [
            out[:, span].astype(jnp.float32)
            * jnp.transpose(jnp.broadcast_to(share[head : head + 1, :], (HD, rows)))
            for out, share in zip(outs, shares)
        ]
        out_ref[:, span] = functools.reduce(jnp.add, terms).astype(out_ref.dtype)


def merge(parts, kv_heads):
    count = len(parts)
    rows, width = parts[0][0].shape
    group = width // HD // kv_heads
    wide = pl.BlockSpec((rows, group * HD), lambda g: (0, g))
    return pl.pallas_call(
        functools.partial(merge_kernel, count, group),
        grid=(kv_heads,),
        in_specs=[pl.BlockSpec((1, 2, group, rows), lambda g: (g, 0, 0, 0))] * count + [wide] * count,
        out_specs=wide,
        out_shape=jax.ShapeDtypeStruct((rows, width), jnp.bfloat16),
        compiler_params=pltpu.CompilerParams(vmem_limit_bytes=ATTEND_GRANT),
        name="merge",
    )(*[stat for _, stat in parts], *[out for out, _ in parts])


def peers_of(me_a, me_b, n, m):
    peers = [{"ba": lax.rem(me_b + k, m)} for k in range(1, m)]
    peers += [{"aa": lax.rem(me_a + hop, n)} for hop in range(2, n, 2)]
    return peers + [{"aa": partner_of(me_a)}]


def partner_of(me_a):
    return me_a + 1 - 2 * lax.rem(me_a, 2)


def meet(peers):
    barrier = pltpu.get_barrier_semaphore()
    for peer in peers:
        pl.semaphore_signal(barrier, inc=1, device_id=peer, device_id_type=pl.DeviceIdType.MESH)
    pl.semaphore_wait(barrier, len(peers))


def remote(source, target, send, receive, peer):
    copy = pltpu.make_async_remote_copy(
        src_ref=source,
        dst_ref=target,
        send_sem=send,
        recv_sem=receive,
        device_id=peer,
        device_id_type=pl.DeviceIdType.MESH,
    )
    copy.start()
    return copy


def dispatch_kernel(local, n, m, packed, out, own_sem, z_send, z_recv, x_send, x_recv, c_send, c_recv):
    me_a, me_b = lax.axis_index("aa"), lax.axis_index("ba")
    slots, columns = packed.shape[1], packed.shape[2]
    meet(peers_of(me_a, me_b, n, 1 if local else m))

    def index(k):
        return k if local else lax.rem(me_b - k + m, m)

    def place(b, a):
        if len(out.shape) == 3:
            return out.at[a, pl.ds(pl.multiple_of(b * slots, slots), slots)]
        return out.at[
            pl.ds(pl.multiple_of(b * slots, slots), slots),
            pl.ds(pl.multiple_of(a * columns, columns), columns),
        ]

    own = []
    for k in range(m if local else 1):
        own.append(pltpu.make_async_copy(packed.at[index(k)], place(index(k), me_a), own_sem.at[k]))
        own[k].start()
    over_z = [None]
    for k in range(1, 1 if local else m):
        to = lax.rem(me_b + k, m)
        over_z.append(
            remote(packed.at[to], place(me_b, me_a), z_send.at[k], z_recv.at[k], {"ba": to})
        )
    partner = partner_of(me_a)
    over_x, over_c = {}, {}

    def forward(k):
        b = index(k)
        for j, hop in enumerate(range(2, n, 2), 1):
            over_x[k, j].wait_recv()
            block = place(b, lax.rem(me_a - hop + n, n))
            over_c[k, j] = remote(
                block, block, c_send.at[k, j], c_recv.at[k, j], {"aa": partner}
            )

    for k in range(m):
        if k < len(own):
            own[k].wait()
        else:
            over_z[k].wait_recv()
        block = place(index(k), me_a)
        for j, hop in enumerate(range(2, n, 2), 1):
            over_x[k, j] = remote(
                block,
                block,
                x_send.at[k, j],
                x_recv.at[k, j],
                {"aa": lax.rem(me_a + hop, n)},
            )
        over_c[k, 0] = remote(block, block, c_send.at[k, 0], c_recv.at[k, 0], {"aa": partner})
        if k > 0:
            forward(k - 1)
    forward(m - 1)
    for copy in over_c.values():
        copy.wait_recv()
    for copy in over_z[1:] + list(over_x.values()) + list(over_c.values()):
        copy.wait_send()


def dispatch(packed, local, m, name, number):
    n = lax.axis_size("aa")
    columns = packed.shape[1]
    rows = packed.shape[0] // m
    half = n // 2
    sems = [pltpu.SemaphoreType.DMA((m,))] * 2 + [pltpu.SemaphoreType.DMA((m, half))] * 4
    flat = columns % LANES == 0 and not local
    shape = (m * rows, n * columns) if flat else (n, m * rows, columns)
    out = pl.pallas_call(
        functools.partial(dispatch_kernel, local, n, m),
        out_shape=jax.ShapeDtypeStruct(shape, packed.dtype),
        in_specs=[pl.BlockSpec(memory_space=pltpu.VMEM)],
        out_specs=pl.BlockSpec(memory_space=pltpu.VMEM),
        scratch_shapes=[pltpu.SemaphoreType.DMA((m,))] + sems,
        compiler_params=pltpu.CompilerParams(
            collective_id=number, has_side_effects=True, vmem_limit_bytes=24 * 1024 * 1024
        ),
        name=name,
    )(packed.reshape(m, rows, columns))
    if local:
        return out.reshape(n * m * rows, columns)
    return out if flat else out.transpose(1, 0, 2).reshape(m * rows, n * columns)


def combine_kernel(
    n, m, part, out, near, summed, far, total, own_sem, z_send, z_recv, x_send, x_recv, c_send, c_recv
):
    me_a, me_b = lax.axis_index("aa"), lax.axis_index("ba")
    slots, columns = out.shape[1], out.shape[2]
    meet(peers_of(me_a, me_b, n, m))
    partner = partner_of(me_a)

    def piece(k, a):
        b = lax.rem(me_b + k, m)
        if len(part.shape) == 3:
            return part.at[a, pl.ds(pl.multiple_of(b * slots, slots), slots)]
        return part.at[
            pl.ds(pl.multiple_of(b * slots, slots), slots),
            pl.ds(pl.multiple_of(a * columns, columns), columns),
        ]

    order = list(range(1, m)) + [0]
    over_c, over_x = {}, {}
    over_z = [None] * m
    for k in order:
        for j in range(n // 2):
            over_c[k, j] = remote(
                piece(k, lax.rem(partner + 2 * j, n)),
                near.at[k, j],
                c_send.at[k, j],
                c_recv.at[k, j],
                {"aa": partner},
            )

    def join(k, j):
        over_c[k, j].wait_recv()
        mine = piece(k, lax.rem(me_a + 2 * j, n))
        return mine[...].astype(jnp.float32) + near[k, j].astype(jnp.float32)

    def finish(k):
        value = join(k, 0)
        for j in range(1, n // 2):
            over_x[k, j].wait_recv()
            value = value + far[k, j].astype(jnp.float32)
        total[k] = value.astype(total.dtype)
        if k == 0:
            copy = pltpu.make_async_copy(total.at[0], out.at[me_b], own_sem)
            copy.start()
            copy.wait()
        else:
            over_z[k] = remote(
                total.at[k],
                out.at[me_b],
                z_send.at[k],
                z_recv.at[k],
                {"ba": lax.rem(me_b + k, m)},
            )

    for k in order:
        for j in range(1, n // 2):
            summed[k, j] = join(k, j).astype(summed.dtype)
            over_x[k, j] = remote(
                summed.at[k, j],
                far.at[k, j],
                x_send.at[k, j],
                x_recv.at[k, j],
                {"aa": lax.rem(me_a + 2 * j, n)},
            )
    for k in order:
        finish(k)
    for copy in over_z[1:]:
        copy.wait_recv()
    for copy in over_z[1:] + list(over_x.values()) + list(over_c.values()):
        copy.wait_send()


def combine(part):
    n, m = lax.axis_size("aa"), lax.axis_size("ba")
    rows, columns = part.shape[0] // m, part.shape[1] // n
    if columns % LANES:
        part = part.reshape(m * rows, n, columns).transpose(1, 0, 2)
    half = n // 2
    sems = [pltpu.SemaphoreType.DMA((m,))] * 2 + [pltpu.SemaphoreType.DMA((m, half))] * 4
    block = pltpu.VMEM((m, half, rows, columns), part.dtype)
    out = pl.pallas_call(
        functools.partial(combine_kernel, n, m),
        out_shape=jax.ShapeDtypeStruct((m, rows, columns), part.dtype),
        in_specs=[pl.BlockSpec(memory_space=pltpu.VMEM)],
        out_specs=pl.BlockSpec(memory_space=pltpu.VMEM),
        scratch_shapes=[block, block, block, pltpu.VMEM((m, rows, columns), part.dtype)]
        + [pltpu.SemaphoreType.DMA]
        + sems,
        compiler_params=pltpu.CompilerParams(
            collective_id=2, has_side_effects=True, vmem_limit_bytes=40 * 1024 * 1024
        ),
        name="combine",
    )(part)
    return out.reshape(m * rows, columns)


def experts_kernel(
    n,
    m,
    packed,
    gate_hbm,
    up_hbm,
    down_hbm,
    out,
    inputs,
    gate_w,
    up_w,
    down_w,
    sums,
    act,
    part,
    near,
    summed,
    far,
    total,
    load_sem,
    own_sem,
    z_send,
    z_recv,
    x_send,
    x_recv,
    c_send,
    c_recv,
    f_send,
    f_recv,
    bz_send,
    bz_recv,
    bx_send,
    bx_recv,
    bc_send,
    bc_recv,
):
    me_a, me_b = lax.axis_index("aa"), lax.axis_index("ba")
    slots, columns = packed.shape[1], packed.shape[2]
    width = n * columns
    hidden = gate_w.shape[1]
    across, partner = flip(me_a, 2), flip(me_a, 1)
    order = [0, 2, 1, 3]
    block_of = [flip(me_b, way) for way in order]

    loads = []
    for at, (source, target) in enumerate(
        ((gate_hbm, gate_w), (up_hbm, up_w), (down_hbm, down_w))
    ):
        piece = target.shape[0] // LOADS
        for i in range(LOADS):
            rows = pl.ds(i * piece, piece)
            loads.append(
                pltpu.make_async_copy(source.at[0, rows], target.at[rows], load_sem.at[at, i])
            )
            loads[-1].start()
    meet([{"ba": block_of[k]} for k in range(1, m)] + [{"aa": across}, {"aa": partner}])

    def place(k, a):
        return inputs.at[
            k * slots : (k + 1) * slots, pl.ds(pl.multiple_of(a * columns, columns), columns)
        ]

    over_z, over_x, over_c, over_f = {}, {}, {}, {}
    own = pltpu.make_async_copy(packed.at[me_b], place(0, me_a), own_sem)
    for k in range(1, m):
        over_z[k] = remote(
            packed.at[block_of[k]], place(k, me_a), z_send.at[k], z_recv.at[k], {"ba": block_of[k]}
        )

    def spread(k):
        if k:
            over_z[k].wait_recv()
        block = place(k, me_a)
        source = block if k else packed.at[me_b]
        over_x[k] = remote(source, block, x_send.at[k], x_recv.at[k], {"aa": across})
        over_c[k] = remote(source, block, c_send.at[k], c_recv.at[k], {"aa": partner})

    def forward(k):
        over_x[k].wait_recv()
        block = place(k, across)
        over_f[k] = remote(block, block, f_send.at[k], f_recv.at[k], {"aa": partner})

    def dots(pair, half, side, finish):
        rows = slice(2 * pair * slots, 2 * (pair + 1) * slots)
        if side is None:
            deep = slice(0, width)
        else:
            deep = pl.ds(pl.multiple_of(side * (width // 2), width // 2), width // 2)

        @pl.loop(0, hidden // 2 // TILE)
        def _(i):
            span = pl.ds(pl.multiple_of(half * (hidden // 2) + i * TILE, TILE), TILE)
            x = inputs[rows, deep]
            gate = jnp.dot(x, gate_w[deep, span], preferred_element_type=jnp.float32)
            up = jnp.dot(x, up_w[deep, span], preferred_element_type=jnp.float32)
            if not finish:
                sums[0, :, span] = gate
                sums[1, :, span] = up
                return
            if side is not None:
                gate = gate + sums[0, :, span]
                up = up + sums[1, :, span]
            act[rows, span] = (jax.nn.silu(gate) * up).astype(jnp.bfloat16)

    back_c, back_x, back_z = {}, {}, {}

    def lower(pair, a):
        rows = slice(2 * pair * slots, 2 * (pair + 1) * slots)

        @pl.loop(0, columns // TILE)
        def _(i):
            span = pl.ds(pl.multiple_of(a * columns + i * TILE, TILE), TILE)
            part[rows, span] = jnp.dot(
                act[rows, :], down_w[:, span], preferred_element_type=jnp.float32
            ).astype(jnp.bfloat16)

    def piece(k, a):
        return part.at[
            k * slots : (k + 1) * slots, pl.ds(pl.multiple_of(a * columns, columns), columns)
        ]

    def hand(k, j, a):
        back_c[k, j] = remote(
            piece(k, a), near.at[k, j], bc_send.at[k, j], bc_recv.at[k, j], {"aa": partner}
        )

    def join(k, j, a, h):
        rows = slice(h * slots // 2, (h + 1) * slots // 2)
        mine = part[
            k * slots + rows.start : k * slots + rows.stop,
            pl.ds(pl.multiple_of(a * columns, columns), columns),
        ]
        return rows, mine.astype(jnp.float32) + near[k, j, rows].astype(jnp.float32)

    def cross(k):
        back_c[k, 1].wait_recv()
        for h in range(2):
            rows, value = join(k, 1, across, h)
            summed[k, rows] = value.astype(summed.dtype)
            back_x[k, h] = remote(
                summed.at[k, rows],
                far.at[k, rows],
                bx_send.at[k, h],
                bx_recv.at[k, h],
                {"aa": across},
            )

    def finish(k):
        back_c[k, 0].wait_recv()
        for h in range(2):
            rows, value = join(k, 0, me_a, h)
            back_x[k, h].wait_recv()
            value = value + far[k, rows].astype(jnp.float32)
            if k == 0:
                out[me_b, rows] = value.astype(out.dtype)
            else:
                total[k, rows] = value.astype(total.dtype)
                back_z[k, h] = remote(
                    total.at[k, rows],
                    out.at[me_b, rows],
                    bz_send.at[k, h],
                    bz_recv.at[k, h],
                    {"ba": block_of[k]},
                )

    def descend(pair):
        first, second = 2 * pair + 1, 2 * pair
        lower(pair, flip(partner, 2))
        hand(first, 1, flip(partner, 2))
        hand(second, 1, flip(partner, 2))
        lower(pair, across)
        cross(first)
        cross(second)
        lower(pair, partner)
        hand(first, 0, partner)
        hand(second, 0, partner)
        lower(pair, me_a)

    spread(0)
    own.start()
    forward(0)
    spread(1)
    for copy in loads[: 2 * LOADS]:
        copy.wait()
    own.wait()
    over_c[0].wait_recv()
    over_c[1].wait_recv()
    side = me_a // 2
    dots(0, 0, side, False)
    dots(0, 1, side, False)
    spread(2)
    forward(1)
    over_f[0].wait_recv()
    over_f[1].wait_recv()
    dots(0, 0, 1 - side, True)
    dots(0, 1, 1 - side, True)
    spread(3)
    forward(2)
    for copy in loads[2 * LOADS :]:
        copy.wait()
    descend(0)
    forward(3)
    for k in (2, 3):
        over_c[k].wait_recv()
        over_f[k].wait_recv()
    dots(1, 0, None, True)
    finish(1)
    dots(1, 1, None, True)
    finish(0)
    descend(1)
    finish(3)
    finish(2)
    for copy in back_z.values():
        copy.wait_recv()
    for group in (over_z, over_x, over_c, over_f, back_c, back_x, back_z):
        for copy in group.values():
            copy.wait_send()


def flip(index, way):
    for bit in (1, 2):
        if way & bit:
            index = index + bit - 2 * bit * lax.rem(index // bit, 2)
    return index


def run_experts(packed, gate_w, up_w, down_w):
    n, m = lax.axis_size("aa"), lax.axis_size("ba")
    rows, columns = packed.shape[1:]
    depth, hidden = gate_w.shape[1:]
    block = pltpu.VMEM((m, rows, columns), jnp.bfloat16)
    one, two = pltpu.SemaphoreType.DMA((m,)), pltpu.SemaphoreType.DMA((m, 2))
    out = pl.pallas_call(
        functools.partial(experts_kernel, n, m),
        out_shape=jax.ShapeDtypeStruct((m, rows, columns), jnp.bfloat16),
        in_specs=[pl.BlockSpec(memory_space=pl.ANY)] * 4,
        out_specs=pl.BlockSpec(memory_space=pltpu.VMEM),
        scratch_shapes=[
            pltpu.VMEM((m * rows, n * columns), jnp.bfloat16),
            pltpu.VMEM((depth, hidden), jnp.bfloat16),
            pltpu.VMEM((depth, hidden), jnp.bfloat16),
            pltpu.VMEM((hidden, n * columns), jnp.bfloat16),
            pltpu.VMEM((2, 2 * rows, hidden), jnp.float32),
            pltpu.VMEM((m * rows, hidden), jnp.bfloat16),
            pltpu.VMEM((m * rows, n * columns), jnp.bfloat16),
            pltpu.VMEM((m, 2, rows, columns), jnp.bfloat16),
            block,
            block,
            block,
            pltpu.SemaphoreType.DMA((3, LOADS)),
            pltpu.SemaphoreType.DMA,
        ]
        + [one] * 8
        + [two] * 6,
        compiler_params=pltpu.CompilerParams(
            collective_id=1, has_side_effects=True, vmem_limit_bytes=EXPERTS_GRANT
        ),
        name="experts",
    )(packed, gate_w, up_w, down_w)
    return out.reshape(m * rows, columns)


def plain_experts(packed, gate_w, up_w, down_w):
    piece = dispatch(packed, False, lax.axis_size("ba"), "dispatch", 1)
    gate_part = jnp.dot(piece, gate_w, preferred_element_type=jnp.float32)
    up_part = jnp.dot(piece, up_w, preferred_element_type=jnp.float32)
    act = (jax.nn.silu(gate_part) * up_part).astype(jnp.bfloat16)
    return combine(jnp.dot(act, down_w, preferred_element_type=jnp.float32).astype(jnp.bfloat16))


def project_kernel(
    n,
    m,
    own,
    weight_hbm,
    residual_hbm,
    gain,
    router,
    ids,
    places,
    hidden_hbm,
    packed_hbm,
    gate_hbm,
    hidden,
    packed,
    gate,
    rows_in,
    weight,
    residual,
    up,
    down,
    leaving,
    value,
    stats,
    normed,
    mix,
    placing,
    load_sem,
    store_sem,
    x_send,
    x_recv,
    c_send,
    c_recv,
    f_send,
    f_recv,
    u_send,
    u_recv,
    d_send,
    d_recv,
    s_send,
    s_recv,
):
    me_a, me_b = lax.axis_index("aa"), lax.axis_index("ba")
    rows, columns = hidden.shape
    experts = router.shape[0]
    slots = packed.shape[1]
    part = rows // PARTS
    across, partner = flip(me_a, 2), flip(me_a, 1)
    loads = [
        pltpu.make_async_copy(weight_hbm, weight, load_sem.at[0]),
        pltpu.make_async_copy(residual_hbm, residual, load_sem.at[1]),
        pltpu.make_async_copy(own, rows_in.at[0], load_sem.at[2]),
    ]
    for copy in loads:
        copy.start()
    meet(
        [{"ba": lax.rem(me_b + k, m)} for k in range(1, m)]
        + [{"aa": flip(me_a, way)} for way in range(1, n)]
    )

    def cut(c):
        return pl.ds(pl.multiple_of(c * part, part), part)

    def pass_on(slot, target, sends, receives, peer, c):
        return pltpu.make_async_remote_copy(
            src_ref=(own if target < 3 else rows_in.at[slot]).at[cut(c)],
            dst_ref=rows_in.at[target, cut(c)],
            send_sem=sends.at[c],
            recv_sem=receives.at[c],
            device_id={"aa": peer},
            device_id_type=pl.DeviceIdType.MESH,
        )

    over_x = functools.partial(pass_on, 0, 2, x_send, x_recv, across)
    over_c = functools.partial(pass_on, 0, 1, c_send, c_recv, partner)
    over_f = functools.partial(pass_on, 2, 3, f_send, f_recv, partner)
    for c in range(PARTS):
        over_x(c).start()
    for c in range(PARTS):
        over_c(c).start()
    half, low = me_b // 2, lax.rem(me_b, 2)
    order = [3 - 3 * half, 2 - half, 2 * half + 1 - low, me_b]

    def climb(b, c, target):
        return pltpu.make_async_remote_copy(
            src_ref=leaving.at[b, cut(c)],
            dst_ref=up.at[b, cut(c)],
            send_sem=u_send.at[b, c],
            recv_sem=u_recv.at[b, c],
            device_id={"ba": target},
            device_id_type=pl.DeviceIdType.MESH,
        )

    def sink(b, c, target):
        return pltpu.make_async_remote_copy(
            src_ref=leaving.at[b, cut(c)],
            dst_ref=down.at[b, cut(c)],
            send_sem=d_send.at[b, c],
            recv_sem=d_recv.at[b, c],
            device_id={"ba": target},
            device_id_type=pl.DeviceIdType.MESH,
        )

    above, below = lax.rem(me_b + 1, m), lax.rem(me_b + m - 1, m)
    for copy in (loads[2], loads[0]):
        copy.wait()

    def step(at, c):
        b = order[at]
        slot = lax.rem(b // 2 + me_a // 2, 2) * 2 + lax.rem(b + me_a, 2)
        value[...] = jnp.dot(
            rows_in[slot, cut(c), :], weight[...], preferred_element_type=jnp.float32
        )

        @pl.when((b >= me_b) & (me_b > 0))
        def _():
            climb(b, c, above).wait_recv()
            value[...] += up[b, cut(c), :].astype(jnp.float32)

        @pl.when((b <= me_b) & (me_b < m - 1))
        def _():
            sink(b, c, below).wait_recv()
            value[...] += down[b, cut(c), :].astype(jnp.float32)

        if at == m - 1:
            hidden[cut(c), :] = residual[cut(c), :].astype(jnp.float32) + value[...]
            return
        leaving[b, cut(c), :] = value[...].astype(leaving.dtype)

        @pl.when(b > me_b)
        def _():
            climb(b, c, above).start()

        @pl.when(b < me_b)
        def _():
            sink(b, c, below).start()

    place = jnp.where(places[...] >= 0, ids[...] * slots + places[...], -1)
    placing[...] = (
        lax.broadcasted_iota(jnp.int32, placing.shape, 0) == place
    ).astype(jnp.bfloat16)
    for c in range(PARTS):
        over_c(c).wait_recv()
    edge = (me_b == 0) | (me_b == m - 1)
    early = edge & (order[0] // 2 != me_a // 2)

    @pl.when(early)
    def _():
        @pl.loop(0, EARLY)
        def _(c):
            step(2, c)

    @pl.loop(0, PARTS)
    def _(c):
        over_x(c).wait_recv()
        over_f(c).start()
        over_f(c).wait_recv()
        step(0, c)

    @pl.loop(0, PARTS)
    def _(c):
        step(1, c)

        @pl.when((early & (c < EARLY)) == False)
        def _():
            step(2, c)

    loads[1].wait()

    @pl.loop(0, PARTS)
    def _(c):
        step(3, c)
        kept = hidden[cut(c), :]
        lane = lax.broadcasted_iota(jnp.int32, (part, LANES), 1)
        square = jnp.sum(kept * kept, axis=1, keepdims=True)
        found = jnp.where(lane == experts, square, 0.0)
        scaled = kept * gain[...]
        for e in range(experts):
            logit = jnp.sum(scaled * router[e : e + 1, :], axis=1, keepdims=True)
            found = jnp.where(lane == e, logit, found)
        mix[cut(c), :] = found

    stores = [pltpu.make_async_copy(hidden, hidden_hbm, store_sem.at[m])]
    stores[0].start()
    stats[0] = jnp.transpose(mix[...])[: stats.shape[1], :]
    over_s = [
        remote(
            stats.at[0],
            stats.at[way],
            s_send.at[way],
            s_recv.at[way],
            {"aa": flip(me_a, way)},
        )
        for way in range(1, n)
    ]
    for copy in over_s:
        copy.wait_recv()
    sums = functools.reduce(jnp.add, [stats[way] for way in range(n)])
    inverse = 1.0 / jnp.sqrt(sums[experts : experts + 1, :] / (n * columns) + EPSILON)
    chosen = ids[...] == lax.broadcasted_iota(jnp.int32, (experts, rows), 0)
    gate[...] = jnp.sum(
        jnp.where(chosen, jax.nn.sigmoid(sums[:experts, :] * inverse), 0.0), axis=0, keepdims=True
    )
    stores.append(pltpu.make_async_copy(gate, gate_hbm, store_sem.at[m + 1]))
    stores[-1].start()
    spread = jnp.transpose(jnp.broadcast_to(inverse, (LANES, rows)))
    for at in range(0, columns, LANES):
        span = slice(at, at + LANES)
        normed[:, span] = (hidden[:, span] * spread * gain[:, span]).astype(jnp.bfloat16)
    for b in range(m):
        packed[b] = jnp.dot(
            placing[b * slots : (b + 1) * slots, :],
            normed[...],
            preferred_element_type=jnp.float32,
        ).astype(packed.dtype)
        stores.append(pltpu.make_async_copy(packed.at[b], packed_hbm.at[b], store_sem.at[b]))
        stores[-1].start()
    for copy in over_s:
        copy.wait_send()

    @pl.loop(0, PARTS)
    def _(c):
        for copy in (over_x, over_c, over_f):
            copy(c).wait_send()
        for at in range(m - 1):

            @pl.when(order[at] > me_b)
            def _(b=order[at], c=c):
                climb(b, c, above).wait_send()

            @pl.when(order[at] < me_b)
            def _(b=order[at], c=c):
                sink(b, c, below).wait_send()

    for copy in stores:
        copy.wait()


def project(own, weight, residual, gain, router, ids, places):
    n, m = lax.axis_size("aa"), lax.axis_size("ba")
    rows, columns = residual.shape
    experts = router.shape[1]
    slots = 2 * rows // experts
    block = pltpu.VMEM((m, rows, columns), jnp.bfloat16)
    one, two = pltpu.SemaphoreType.DMA((PARTS,)), pltpu.SemaphoreType.DMA((m, PARTS))
    vmem, anywhere = pl.BlockSpec(memory_space=pltpu.VMEM), pl.BlockSpec(memory_space=pl.ANY)
    return pl.pallas_call(
        functools.partial(project_kernel, n, m),
        out_shape=[
            jax.ShapeDtypeStruct((rows, columns), jnp.float32),
            jax.ShapeDtypeStruct((m, slots, columns), jnp.bfloat16),
            jax.ShapeDtypeStruct((1, rows), jnp.float32),
        ],
        in_specs=[anywhere, anywhere, anywhere, vmem, vmem, vmem, vmem],
        out_specs=[anywhere] * 3,
        scratch_shapes=[
            pltpu.VMEM((rows, columns), jnp.float32),
            pltpu.VMEM((m, slots, columns), jnp.bfloat16),
            pltpu.VMEM((1, rows), jnp.float32),
            pltpu.VMEM((n, rows, own.shape[1]), jnp.bfloat16),
            pltpu.VMEM(weight.shape, jnp.bfloat16),
            pltpu.VMEM((rows, columns), jnp.bfloat16),
            block,
            block,
            block,
            pltpu.VMEM((rows // PARTS, columns), jnp.float32),
            pltpu.VMEM((n, 8, rows), jnp.float32),
            pltpu.VMEM((rows, columns), jnp.bfloat16),
            pltpu.VMEM((rows, LANES), jnp.float32),
            pltpu.VMEM((m * slots, rows), jnp.bfloat16),
            pltpu.SemaphoreType.DMA((3,)),
            pltpu.SemaphoreType.DMA((m + 2,)),
        ]
        + [one] * 6
        + [two] * 4
        + [pltpu.SemaphoreType.DMA((n,))] * 2,
        compiler_params=pltpu.CompilerParams(
            collective_id=4, has_side_effects=True, vmem_limit_bytes=PROJECT_GRANT
        ),
        name="project",
    )(
        own,
        weight,
        residual,
        gain.reshape(1, columns),
        router.T,
        ids.reshape(1, rows),
        places.reshape(1, rows),
    )


def placing_of(expert_ids, expert_slots, experts):
    slot_count = 2 * expert_ids.shape[0] // experts
    combined = expert_ids * slot_count + expert_slots
    placing = (
        combined[:, None] == lax.broadcasted_iota(jnp.int32, (1, experts * slot_count), 1)
    ) & (expert_slots[:, None] >= 0)
    return placing.astype(jnp.bfloat16)


def plain_project(
    own, out_weight, residual, norm_gain, router_weight, expert_ids, expert_slots
):
    attended = dispatch(own, True, 4 if own.shape[0] % 64 == 0 else 1, "gather", 3)
    hidden = residual.astype(jnp.float32) + lax.psum_scatter(
        jnp.dot(attended, out_weight, preferred_element_type=jnp.float32).astype(jnp.bfloat16),
        "ba",
        scatter_dimension=0,
        tiled=True,
    ).astype(jnp.float32)
    scaled = hidden * norm_gain
    sums = lax.psum(
        jnp.concatenate(
            [
                jnp.dot(scaled, router_weight, precision=lax.Precision.HIGHEST),
                jnp.sum(hidden * hidden, axis=1, keepdims=True),
            ],
            axis=1,
        ),
        "aa",
    )
    inverse = 1.0 / jnp.sqrt(sums[:, -1] / D + EPSILON)
    normed = scaled * inverse[:, None]
    logits = sums[:, :-1] * inverse[:, None]
    experts = router_weight.shape[1]
    chosen = expert_ids[:, None] == lax.broadcasted_iota(jnp.int32, (1, experts), 1)
    gate = jnp.sum(jnp.where(chosen, jax.nn.sigmoid(logits), 0.0), axis=1)
    expert_in = normed.astype(jnp.bfloat16)
    placing = placing_of(expert_ids, expert_slots, experts)
    packed = lax.dot_general(
        placing, expert_in, (((0,), (0,)), ((), ())), preferred_element_type=jnp.float32
    ).astype(jnp.bfloat16)
    return hidden, packed, gate


def on_device(
    query,
    keys,
    values,
    cache_lengths,
    residual,
    out_weight,
    norm_gain,
    router_weight,
    expert_ids,
    expert_slots,
    expert_gate,
    expert_up,
    expert_down,
):
    own = span_attention(query, keys, values, cache_lengths)
    n, m = lax.axis_size("aa"), lax.axis_size("ba")
    experts = router_weight.shape[1]
    rows, columns = residual.shape
    if n == 4 and m == 4 and experts == m and own.shape[0] == rows and columns % LANES == 0:
        hidden, packed, gate = project(
            own, out_weight, residual, norm_gain, router_weight, expert_ids, expert_slots
        )
        returned = run_experts(packed, expert_gate, expert_up, expert_down)
        gate = gate[0]
    else:
        hidden, packed, gate = plain_project(
            own, out_weight, residual, norm_gain, router_weight, expert_ids, expert_slots
        )
        returned = plain_experts(packed, expert_gate[0], expert_up[0], expert_down[0])
    placing = placing_of(expert_ids, expert_slots, experts)
    from_experts = jnp.dot(placing, returned, preferred_element_type=jnp.float32)
    return (hidden + gate[:, None] * from_experts).astype(jnp.bfloat16)


def solution(mesh):
    return jax.shard_map(
        on_device,
        mesh=mesh,
        in_specs=(
            P(("ga", "aa"), "ba"),
            P(("ga", "aa"), "ba"),
            P(("ga", "aa"), "ba"),
            P(("ga", "aa")),
            P(("ga", "ba"), "aa"),
            P("ba", "aa"),
            P("aa"),
            P("aa", None),
            P(("ga", "ba")),
            P(("ga", "ba")),
            P("ba", None, "aa"),
            P("ba", None, "aa"),
            P("ba", "aa", None),
        ),
        out_specs=P(("ga", "ba"), "aa"),
        check_vma=False,
    )
```
